128 devices in a mesh: atom: 8 (over x, core), tm: 16 (over z, y).
Axes of the slice: x: 4, y: 4, z: 4, core: 2. Of those that a mesh axis runs over, the one named last changes fastest.
Arguments:
- positions: int32 [128, 3, 16384], P('tm', None, 'atom'), may hold values from 0 to 131071, as said below
- velocity: bfloat16 [128, 3, 16384], P('tm', None, 'atom'), may hold values from -5 to 5
Outputs:
- correlation: float32 [4, 16, 32768], P(None, None, ('atom', 'tm'))
The draws below stay inside these ranges and needn't reach their ends.
Inputs may be any that keep to these rules, and one draw needn't show every extreme that they name: `positions`: along each axis an atom's coordinate changes between consecutive frames by at most 1536 lattice points, counted modulo 131072.
All inputs are finite; a program needn't handle non-finite values.
Results may differ from the reference program's by a relative error of at most 0.00075.
Values may be sent and summed in bfloat16 or wider, within the bound.
No kernel may reach another device: no remote copies, remote signals or barrier semaphores. Data moves between devices by JAX's collectives and lax.ppermute only.
A program may use at most 128 MiB of HBM per device.

```python
import math
import jax
import jax.numpy as jnp
from jax import lax

KX = 32
KY = 32
KZ = 32
LAGS = 16
LATTICE = 131072
STEP = 1536
ATOMS = 16384
FRAMES = 128


def walk_steps(key):
    walk_key = jax.random.fold_in(key, 11)
    first_key, step_key, speed_key = jax.random.split(walk_key, 3)
    anchor = jax.random.randint(first_key, (1, 3, ATOMS), 0, LATTICE, dtype=jnp.int32)
    displacement = jax.random.randint(step_key, (FRAMES, 3, ATOMS), -STEP, STEP + 1, dtype=jnp.int32)
    return (anchor, displacement, speed_key)


def draw_positions(key, part):
    anchor, displacement, speed_key = walk_steps(key)
    travelled = jnp.cumsum(displacement, 0) - displacement
    return (anchor + travelled) % LATTICE


def draw_velocity(key, part):
    anchor, displacement, speed_key = walk_steps(key)
    drift_key = jax.random.fold_in(speed_key, 0)
    drift_speed = 0.5 * jnp.clip(jax.random.normal(drift_key, (1, 3, ATOMS), jnp.float32), -4.0, 4.0)
    moving = drift_speed + 0.5 * displacement.astype(jnp.float32) / STEP
    return moving.astype(jnp.bfloat16)


def setup_inputs(seed: int = 0) -> dict:
    splits = jax.random.split(jax.random.key(seed), 3)
    return {
        "positions": draw_positions(jax.random.fold_in(splits[2], 71), 0),
        "velocity": draw_velocity(jax.random.fold_in(splits[2], 71), 0),
    }


def wave_numbers(number, offset, extent):
    counter = jnp.arange(number, dtype=jnp.int32) + offset
    return counter - extent // 2 + (counter >= extent // 2).astype(jnp.int32)


def phase_pair(coords, numbers):
    folded = (numbers[None, :, None] * coords[:, None, :]) % LATTICE
    angles = folded.astype(jnp.float32) * (2.0 * math.pi / LATTICE)
    return jnp.cos(angles), jnp.sin(angles)


def operands(positions, velocity, kx_first, kx_number):
    frame_count, atom_count = positions.shape[0], positions.shape[2]
    cos_x, sin_x = phase_pair(positions[:, 0], wave_numbers(kx_number, kx_first, KX))
    cos_y, sin_y = phase_pair(positions[:, 1], wave_numbers(KY, 0, KY))
    cos_z, sin_z = phase_pair(positions[:, 2], wave_numbers(KZ, 0, KZ))
    real_xy = cos_x[:, :, None] * cos_y[:, None] - sin_x[:, :, None] * sin_y[:, None]
    imag_xy = cos_x[:, :, None] * sin_y[:, None] + sin_x[:, :, None] * cos_y[:, None]
    left_side = jnp.concatenate([real_xy, imag_xy], 1)
    left_side = left_side.reshape(frame_count, 2 * kx_number * KY, atom_count).astype(jnp.bfloat16)
    weights = jnp.concatenate([jnp.ones((frame_count, 1, atom_count), jnp.float32), velocity.astype(jnp.float32)], 1)
    right_side = jnp.stack([cos_z[:, None] * weights[:, :, None], sin_z[:, None] * weights[:, :, None]], 2)
    right_side = right_side.reshape(frame_count, -1, atom_count).astype(jnp.bfloat16)
    return left_side, right_side


def finish(raw, row_count):
    frame_count = raw.shape[0]
    split = raw.reshape(frame_count, 2, row_count, -1, 2, KZ)
    real_part = split[:, 0, :, :, 0] - split[:, 1, :, :, 1]
    imag_part = split[:, 0, :, :, 1] + split[:, 1, :, :, 0]
    joined = jnp.stack([real_part, imag_part], 3)
    return jnp.transpose(joined, (1, 0, 2, 3, 4)).reshape(row_count, -1)


def mode_rows(positions, velocity, kx_first, kx_number, block_limit):
    frame_count, atom_count = positions.shape[0], positions.shape[2]
    atom_block = math.gcd(atom_count, block_limit)
    row_count = kx_number * KY
    channels = (velocity.shape[1] + 1) * 2 * KZ

    def accumulate(running, block_index):
        pos_block = lax.dynamic_slice_in_dim(positions, block_index * atom_block, atom_block, 2)
        vel_block = lax.dynamic_slice_in_dim(velocity, block_index * atom_block, atom_block, 2)
        left_side, right_side = operands(pos_block, vel_block, kx_first, kx_number)
        product = jnp.einsum("fra,fca->frc", left_side.astype(jnp.float32), right_side.astype(jnp.float32))
        return running + product, None

    initial = jnp.zeros((frame_count, 2 * row_count, channels), jnp.float32)
    running = lax.scan(accumulate, initial, jnp.arange(atom_count // atom_block, dtype=jnp.int32))[0]
    return finish(running, row_count)


def reference(positions, velocity):
    frame_count, atom_count = positions.shape[0], positions.shape[2]

    def one_frame(frame_pair):
        return mode_rows(frame_pair[0][None], frame_pair[1][None], 0, KX, 2048)

    modes = lax.map(one_frame, (positions, velocity))
    modes = modes.reshape(frame_count, KX * KY, -1, 2, KZ)
    results = []
    for lag_index in range(LAGS):
        product = modes[: frame_count - lag_index] * modes[lag_index:]
        results.append(jnp.sum(product, axis=(0, 3)) / (atom_count * (frame_count - lag_index)))
    stacked = jnp.stack(results)
    return jnp.transpose(stacked, (2, 0, 1, 3)).reshape(stacked.shape[2], LAGS, -1)
```

```python
import functools
import math

import jax
import jax.numpy as jnp
from jax import lax
from jax.experimental import pallas as pl
from jax.experimental.pallas import tpu as pltpu
from jax.sharding import PartitionSpec as P

KX = 32
KY = 32
KZ = 32
LAGS = 16
LATTICE = 131072
ATOMS = 16384
FRAMES = 128
HALF = 16
ROWS = 80
SINE = (6.28318516, -41.3416550, 81.6010040, -76.5498338, 39.5367090)


def sine(u):
    square = u * u
    value = jnp.full_like(u, SINE[4])
    for factor in SINE[3::-1]:
        value = value * square + factor
    return value * u


def cos_sin(turns):
    r = turns - jnp.round(turns)
    c = sine(0.25 - jnp.abs(r))
    s = sine(jnp.maximum(jnp.minimum(r, 0.5 - r), -0.5 - r))
    return c, s


def harmonics(c, s):
    twice = c + c
    cs, ss = [c], [s]
    before_c, before_s = jnp.ones_like(c), jnp.zeros_like(s)
    for _ in range(HALF - 1):
        next_c, next_s = twice * cs[-1] - before_c, twice * ss[-1] - before_s
        before_c, before_s = cs[-1], ss[-1]
        cs.append(next_c)
        ss.append(next_s)
    return cs, ss


def build(data, first, table, left, right):
    groups = 16

    def put(row, value):
        table[pl.ds(row, groups, stride=ROWS), :] = value

    turns = [
        (data[2 * a].astype(jnp.float32) * 512.0 + data[2 * a + 1].astype(jnp.float32))
        * (1.0 / LATTICE)
        for a in range(3)
    ]
    c, s = cos_sin(turns[0] * first)
    c1, s1 = cos_sin(turns[0])
    for i in range(4):
        put(2 * i, c)
        put(2 * i + 1, s)
        if i < 3:
            c, s = c * c1 - s * s1, c * s1 + s * c1
    for axis in (1, 2):
        cs, ss = harmonics(*cos_sin(turns[axis]))
        base = 8 + 32 * (axis - 1)
        for w in range(HALF):
            put(base + w, cs[w])
            put(base + HALF + w, ss[w])
    for comp in range(3):
        put(72 + comp, data[6 + comp].astype(jnp.float32))
    for g in range(groups):
        base = g * ROWS
        lanes = slice(g * 128, (g + 1) * 128)
        yc = [table[base + 8 + 8 * b : base + 16 + 8 * b, :] for b in range(2)]
        ys = [table[base + 24 + 8 * b : base + 32 + 8 * b, :] for b in range(2)]
        for i in range(4):
            cx = table[pl.ds(base + 2 * i, 1), :]
            sx = table[pl.ds(base + 2 * i + 1, 1), :]
            for b in range(2):
                cc, sn = cx * yc[b], sx * ys[b]
                cn, sc = cx * ys[b], sx * yc[b]
                plus = jnp.concatenate([cc - sn, cn + sc], 0).astype(jnp.bfloat16)
                minus = jnp.concatenate([cc + sn, sc - cn], 0).astype(jnp.bfloat16)
                row = (i * 4 + 2 + b) * 16
                left[row : row + 16, lanes] = plus
                row = (i * 4 + 1 - b) * 16
                left[row : row + 16, lanes] = minus
        for part in range(2):
            z = table[base + 40 + 16 * part : base + 56 + 16 * part, :]
            for comp in range(4):
                value = z if comp == 0 else z * table[pl.ds(base + 71 + comp, 1), :]
                row = part * 64 + comp * 16
                right[row : row + 16, lanes] = value.astype(jnp.bfloat16)


def modes_kernel(number, first_ref, *refs):
    data, out = refs[:number], refs[number]
    table, left_a, right_a, left_b, right_b, total = refs[number + 1 :]
    first = first_ref[0]
    total[...] = jnp.zeros_like(total)
    operands = ((left_a, right_a), (left_b, right_b))

    def multiply(which):
        left, right = operands[which]
        total[...] += lax.dot_general(
            right[...], left[...], (((1,), (1,)), ((), ())), preferred_element_type=jnp.float32
        )

    for g in range(number):
        build([data[g][0, k] for k in range(9)], first, table, *operands[g % 2])
        multiply(g % 2)
    turned = jnp.transpose(total[...])
    out[...] = turned.reshape(16, 1, 16, 128)


def modes(first, blocks):
    frames = blocks[0].shape[0]
    number = len(blocks)
    spec = pl.BlockSpec((1, 9, 16, 128), lambda f: (f, 0, 0, 0))
    return pl.pallas_call(
        functools.partial(modes_kernel, number),
        grid=(frames,),
        out_shape=jax.ShapeDtypeStruct((16, frames, 16, 128), jnp.float32),
        in_specs=[pl.BlockSpec(memory_space=pltpu.SMEM)] + [spec] * number,
        out_specs=pl.BlockSpec((16, 1, 16, 128), lambda f: (0, f, 0, 0)),
        scratch_shapes=[pltpu.VMEM((16 * ROWS, 128), jnp.float32)]
        + [pltpu.VMEM((256, 2048), jnp.bfloat16), pltpu.VMEM((128, 2048), jnp.bfloat16)] * 2
        + [pltpu.VMEM((128, 256), jnp.float32)],
        compiler_params=pltpu.CompilerParams(dimension_semantics=("arbitrary",)),
        name="modes",
    )(first, *blocks)


def correlate_kernel(flip_ref, series, pick, out, d, e, rows):
    frames = FRAMES
    d[frames:, :, :] = jnp.zeros((LAGS, 8, 128), jnp.float32)
    e[frames:, :, :] = jnp.zeros((LAGS, 8, 128), jnp.float32)

    def split(t, carry):
        values = series[t].astype(jnp.float32)
        real, imag = values[:8], pltpu.roll(values[8:], 64, 1)
        d[t] = real - imag
        e[t] = real + imag
        return carry

    lax.fori_loop(0, frames, split, 0, unroll=8)

    def lags(source):
        def step(t, sums):
            here = source[t]
            return tuple(sums[lag] + here * source[t + lag] for lag in range(LAGS))

        zero = jnp.zeros((8, 128), jnp.float32)
        return lax.fori_loop(0, frames, step, (zero,) * LAGS, unroll=4)

    sums_d, sums_e = lags(d), lags(e)
    for lag in range(LAGS):
        value = (sums_d[lag] + pltpu.roll(sums_e[lag], 64, 1)) * (1.0 / (ATOMS * (frames - lag)))
        rows[lag * 8 : lag * 8 + 8, :] = value
    rows[...] = jnp.dot(
        rows[...], pick[...], precision=lax.Precision.HIGHEST, preferred_element_type=jnp.float32
    )
    flip = flip_ref[0] == 1
    lane = lax.broadcasted_iota(jnp.int32, (LAGS, 128), 1) // 32
    for half in range(2):
        totals = [jnp.zeros((LAGS, 128), jnp.float32) for _ in range(4)]
        for part in range(4):
            w = half * 4 + part
            ahead = rows[pl.ds(w, LAGS, stride=8), :]
            back = rows[pl.ds(7 - w, LAGS, stride=8), :]
            value = jnp.where(flip, back, ahead)
            for comp in range(4):
                shift = (32 * (part - comp)) % 128
                moved = pltpu.roll(value, shift, 1) if shift else value
                totals[comp] = jnp.where(lane == part, moved, totals[comp])
        for comp in range(4):
            out[comp, :, half * 128 : half * 128 + 128] = totals[comp]


def correlate(flip, series):
    lane = jnp.arange(128)
    comp, q = lane // 32, lane % 32
    source = jnp.where(q < 16, 64 + comp * 16 + 15 - q, comp * 16 + q - 16)
    pick = (lane[:, None] == source[None, :]).astype(jnp.float32)
    vmem = pl.BlockSpec(memory_space=pltpu.VMEM)
    return pl.pallas_call(
        correlate_kernel,
        out_shape=jax.ShapeDtypeStruct((4, LAGS, 256), jnp.float32),
        in_specs=[pl.BlockSpec(memory_space=pltpu.SMEM), vmem, vmem],
        out_specs=vmem,
        scratch_shapes=[
            pltpu.VMEM((FRAMES + LAGS, 8, 128), jnp.float32),
            pltpu.VMEM((FRAMES + LAGS, 8, 128), jnp.float32),
            pltpu.VMEM((128, 128), jnp.float32),
        ],
        name="correlate",
    )(flip, series, pick)


def gather_atoms(own):
    sibling = [(i, i ^ 1) for i in range(8)]
    blocks = [own, lax.ppermute(own, "atom", sibling)]
    for step in (1, 3, 2):
        there = lax.ppermute(own, "atom", [(i, (i + 2 * step) % 8) for i in range(8)])
        blocks += [there, lax.ppermute(there, "atom", sibling)]
    return blocks


def per_device(positions, velocity):
    a = lax.axis_index("atom")
    t = lax.axis_index("tm")
    frames = positions.shape[0]
    low = ((positions + 256) & 511) - 256
    high = (positions - low) >> 9
    parts = jnp.stack([high, low], 2).reshape(frames, 6, 16, 128).astype(jnp.bfloat16)
    own = jnp.concatenate([parts, velocity.reshape(frames, 3, 16, 128)], 1)
    first = (4 * a - 16 + (a >= 4)).astype(jnp.float32).reshape(1)
    local = modes(first, gather_atoms(own))
    series = lax.all_to_all(local, "tm", split_axis=0, concat_axis=0, tiled=True)
    flip = (t % 4 < 2).astype(jnp.int32).reshape(1)
    return correlate(flip, series.reshape(FRAMES, 16, 128))


def solution(mesh):
    in_specs = (P("tm", None, "atom"), P("tm", None, "atom"))
    out_specs = P(None, None, ("atom", "tm"))
    return jax.shard_map(
        per_device, mesh=mesh, in_specs=in_specs, out_specs=out_specs, check_vma=False
    )
```

```python
import functools
import math

import jax
import jax.numpy as jnp
from jax import lax
from jax.experimental import pallas as pl
from jax.experimental.pallas import tpu as pltpu
from jax.sharding import PartitionSpec as P

KX = 32
KY = 32
KZ = 32
LAGS = 16
LATTICE = 131072
ATOMS = 16384
FRAMES = 128
HALF = 16
REAL = False
ROWS = 81
SINE = (6.28318516, -41.3416550, 81.6010040, -76.5498338, 39.5367090)


def sine(u):
    square = u * u
    value = jnp.full_like(u, SINE[4])
    for factor in SINE[3::-1]:
        value = value * square + factor
    return value * u


def cos_sin(turns):
    r = turns - jnp.round(turns)
    c = sine(0.25 - jnp.abs(r))
    s = sine(jnp.maximum(jnp.minimum(r, 0.5 - r), -0.5 - r))
    return c, s


def harmonics(c, s):
    twice = c + c
    cs, ss = [c], [s]
    before_c, before_s = jnp.ones_like(c), jnp.zeros_like(s)
    for _ in range(HALF - 1):
        next_c, next_s = twice * cs[-1] - before_c, twice * ss[-1] - before_s
        before_c, before_s = cs[-1], ss[-1]
        cs.append(next_c)
        ss.append(next_s)
    return cs, ss


def fill(data, first, table):
    def put(row, value):
        table[pl.ds(row, 16, stride=ROWS), :] = value

    turns = [
        (data[2 * a].astype(jnp.float32) * 512.0 + data[2 * a + 1].astype(jnp.float32))
        * (1.0 / LATTICE)
        for a in range(3)
    ]
    c, s = cos_sin(turns[0] * first)
    c1, s1 = cos_sin(turns[0])
    for i in range(4):
        put(2 * i, c)
        put(2 * i + 1, s)
        if i < 3:
            c, s = c * c1 - s * s1, c * s1 + s * c1
    for axis in (1, 2):
        cs, ss = harmonics(*cos_sin(turns[axis]))
        base = 8 + 32 * (axis - 1)
        for w in range(HALF):
            put(base + w, cs[w])
            put(base + HALF + w, ss[w])
    for comp in range(3):
        put(72 + comp, data[6 + comp].astype(jnp.float32))


def multiply(table, total):
    for pair in range(8):
        bases = [(2 * pair + k) * ROWS for k in range(2)]

        def rows(start, number):
            return [table[pl.ds(base + start, number), :] for base in bases]

        def wide(parts):
            return jnp.concatenate([p.astype(jnp.bfloat16) for p in parts], 1)

        yc = [rows(8 + 8 * b, 8) for b in range(2)]
        ys = [rows(24 + 8 * b, 8) for b in range(2)]
        left = []
        for i in range(4):
            cx, sx = rows(2 * i, 1), rows(2 * i + 1, 1)
            for b in range(2):
                one, two = [], []
                for k in range(2):
                    cc, sn = cx[k] * yc[b][k], sx[k] * ys[b][k]
                    cn, sc = cx[k] * ys[b][k], sx[k] * yc[b][k]
                    if REAL:
                        one.append(jnp.concatenate([cc, sn], 0))
                        two.append(jnp.concatenate([cn, sc], 0))
                    else:
                        one.append(jnp.concatenate([cc - sn, cn + sc], 0))
                        two.append(jnp.concatenate([cc + sn, sc - cn], 0))
                left += [wide(one), wide(two)]
        right = []
        for part in range(2):
            z = rows(40 + 16 * part, 16)
            right.append(wide(z))
            for comp in range(3):
                u = rows(72 + comp, 1)
                right.append(wide([z[k] * u[k] for k in range(2)]))
        left, right = jnp.concatenate(left, 0), jnp.concatenate(right, 0)
        total = total + lax.dot_general(
            right, left, (((1,), (1,)), ((), ())), preferred_element_type=jnp.float32
        )
    return total


def modes_kernel(number, frames, more, last, first_ref, *refs):
    if more:
        before, refs = refs[0], refs[1:]
    data, out = refs[:number], refs[number]
    table_a, table_b, blocks, *rest = refs[number + 1 :]
    totals = rest[0] if last else out
    first = first_ref[0]
    steps = number * frames
    for g in range(number):
        for f in range(frames):
            blocks[f * number + g] = data[g][f]

    def block(index):
        return [blocks[index, k] for k in range(9)]

    totals[...] = before[...] if more else jnp.zeros_like(totals)
    fill(block(0), first, table_a)

    def step(half, carry):
        now = 2 * half
        frame = now // number
        fill(block(now + 1), first, table_b)
        total = multiply(table_a, totals[frame])
        fill(block(jnp.minimum(now + 2, steps - 1)), first, table_a)
        totals[frame] = multiply(table_b, total)
        return carry

    lax.fori_loop(0, steps // 2, step, 0)
    if not last:
        return
    for f in range(frames):
        total = jnp.transpose(totals[f])
        for i in range(4):
            for b in range(2):
                part = total[64 * i + 32 * b : 64 * i + 32 * b + 32]
                if REAL:
                    cc, sn, cn, sc = part[:8], part[8:16], part[16:24], part[24:]
                    part = jnp.concatenate([cc - sn, cn + sc, cc + sn, sc - cn], 0)
                out[i * 4 + 2 + b, f] = part[:16]
                out[i * 4 + 1 - b, f] = part[16:]


def modes(first, blocks, before=None, part=0, parts=1, last=False):
    frames = blocks[0].shape[0] // parts
    number, more = len(blocks), before is not None
    smem = pl.BlockSpec(memory_space=pltpu.SMEM)
    data = pl.BlockSpec((frames, 9, 16, 128), lambda _: (part, 0, 0, 0))
    sums = pl.BlockSpec((frames, 128, 256), lambda _: (part, 0, 0))
    owned = (16, frames, 16, 128)
    scratch = [
        pltpu.VMEM((16 * ROWS, 128), jnp.float32),
        pltpu.VMEM((16 * ROWS, 128), jnp.float32),
        pltpu.VMEM((number * frames, 9, 16, 128), jnp.bfloat16),
    ]
    work = number * frames * 2048
    return pl.pallas_call(
        functools.partial(modes_kernel, number, frames, more, last),
        grid=(1,),
        out_shape=jax.ShapeDtypeStruct(owned if last else (frames, 128, 256), jnp.float32),
        in_specs=[smem] + [sums] * more + [data] * number,
        out_specs=pl.BlockSpec(owned, lambda _: (0, 0, 0, 0)) if last else sums,
        scratch_shapes=scratch + [pltpu.VMEM((frames, 128, 256), jnp.float32)] * last,
        cost_estimate=pl.CostEstimate(
            flops=work * 256 * 128 * 2, bytes_accessed=work * 18, transcendentals=0
        ),
        name=f"last{part}" if last else f"nearby{int(more)}",
    )(first, *([before] * more), *blocks)


def correlate_kernel(flip_ref, early, late, pick, out, d, e, rows):
    frames = FRAMES
    d[frames:, :, :] = jnp.zeros((LAGS, 8, 128), jnp.float32)
    e[frames:, :, :] = jnp.zeros((LAGS, 8, 128), jnp.float32)

    def split(source, carry):
        for part, series in enumerate((early, late)):
            for f in range(series.shape[1]):
                values = series[source, f].astype(jnp.float32)
                real, imag = values[:8], pltpu.roll(values[8:], 64, 1)
                t = source * 8 + part * early.shape[1] + f
                d[t] = real - imag
                e[t] = real + imag
        return carry

    lax.fori_loop(0, 16, split, 0)

    def lags(source):
        def step(t, sums):
            here = source[t]
            return tuple(sums[lag] + here * source[t + lag] for lag in range(LAGS))

        zero = jnp.zeros((8, 128), jnp.float32)
        return lax.fori_loop(0, frames, step, (zero,) * LAGS, unroll=4)

    sums_d, sums_e = lags(d), lags(e)
    for lag in range(LAGS):
        value = (sums_d[lag] + pltpu.roll(sums_e[lag], 64, 1)) * (1.0 / (ATOMS * (frames - lag)))
        rows[lag * 8 : lag * 8 + 8, :] = value
    rows[...] = jnp.dot(
        rows[...], pick[...], precision=lax.Precision.HIGHEST, preferred_element_type=jnp.float32
    )
    flip = flip_ref[0] == 1
    lane = lax.broadcasted_iota(jnp.int32, (LAGS, 128), 1) // 32
    for half in range(2):
        totals = [jnp.zeros((LAGS, 128), jnp.float32) for _ in range(4)]
        for part in range(4):
            w = half * 4 + part
            ahead = rows[pl.ds(w, LAGS, stride=8), :]
            back = rows[pl.ds(7 - w, LAGS, stride=8), :]
            value = jnp.where(flip, back, ahead)
            for comp in range(4):
                shift = (32 * (part - comp)) % 128
                moved = pltpu.roll(value, shift, 1) if shift else value
                totals[comp] = jnp.where(lane == part, moved, totals[comp])
        for comp in range(4):
            out[comp, :, half * 128 : half * 128 + 128] = totals[comp]


def correlate(flip, early, late):
    lane = jnp.arange(128)
    comp, q = lane // 32, lane % 32
    source = jnp.where(q < 16, 64 + comp * 16 + 15 - q, comp * 16 + q - 16)
    pick = (lane[:, None] == source[None, :]).astype(jnp.float32)
    vmem = pl.BlockSpec(memory_space=pltpu.VMEM)
    return pl.pallas_call(
        correlate_kernel,
        out_shape=jax.ShapeDtypeStruct((4, LAGS, 256), jnp.float32),
        in_specs=[pl.BlockSpec(memory_space=pltpu.SMEM), vmem, vmem, vmem],
        out_specs=vmem,
        scratch_shapes=[
            pltpu.VMEM((FRAMES + LAGS, 8, 128), jnp.float32),
            pltpu.VMEM((FRAMES + LAGS, 8, 128), jnp.float32),
            pltpu.VMEM((128, 128), jnp.float32),
        ],
        name="correlate",
    )(flip, early, late, pick)


def shift(block, by):
    return lax.ppermute(block, "atom", [(i, (i + by) % 8) for i in range(8)])


def swap(block):
    return lax.ppermute(block, "atom", [(i, i ^ 1) for i in range(8)])


def per_device(positions, velocity):
    a = lax.axis_index("atom")
    t = lax.axis_index("tm")
    frames = positions.shape[0]
    low = ((positions + 256) & 511) - 256
    high = (positions - low) >> 9
    parts = jnp.stack([high, low], 2).reshape(frames, 6, 16, 128).astype(jnp.bfloat16)
    own = jnp.concatenate([parts, velocity.reshape(frames, 3, 16, 128)], 1)
    first = (4 * a - 16 + (a >= 4)).astype(jnp.float32).reshape(1)
    left, right, across = shift(own, 2), shift(own, 6), shift(own, 4)
    sums = modes(first, [own, swap(own)])
    left, right, sums = lax.optimization_barrier((left, right, sums))
    far = [swap(left), swap(right)]
    sums = modes(first, [left, right], sums)
    across, sums, *far = lax.optimization_barrier((across, sums, *far))
    far += [across, swap(across)]
    series = []
    for part in range(2):
        local = modes(first, far, sums, part, 2, True)
        series.append(lax.all_to_all(local, "tm", split_axis=0, concat_axis=0, tiled=True))
    flip = (t % 4 < 2).astype(jnp.int32).reshape(1)
    return correlate(flip, *series)


def solution(mesh):
    in_specs = (P("tm", None, "atom"), P("tm", None, "atom"))
    out_specs = P(None, None, ("atom", "tm"))
    return jax.shard_map(
        per_device, mesh=mesh, in_specs=in_specs, out_specs=out_specs, check_vma=False
    )
```

```python
import functools
import math

import jax
import jax.numpy as jnp
from jax import lax
from jax.experimental import pallas as pl
from jax.experimental.pallas import tpu as pltpu
from jax.sharding import PartitionSpec as P

KX = 32
KY = 32
KZ = 32
LAGS = 16
LATTICE = 131072
ATOMS = 16384
FRAMES = 128
HALF = 16
ROWS = 59
SINE = (6.28318516, -41.3416550, 81.6010040, -76.5498338, 39.5367090)


def sine(u):
    square = u * u
    value = jnp.full_like(u, SINE[4])
    for factor in SINE[3::-1]:
        value = value * square + factor
    return value * u


def cos_sin(turns):
    r = turns - jnp.round(turns)
    c = sine(0.25 - jnp.abs(r))
    s = sine(jnp.maximum(jnp.minimum(r, 0.5 - r), -0.5 - r))
    return c, s


def double(c, s):
    return 2.0 * c * c - 1.0, 2.0 * s * c


def harmonics(here, before, twice, number):
    values = [here]
    for _ in range(number - 1):
        values.append(twice * values[-1] - before)
        before = values[-2]
    return values


def fill(data, first, odd, table):
    def put(row, values):
        for k, value in enumerate(values):
            table[pl.ds(row + k, 16, stride=ROWS), :] = value

    x, y, z = (
        (data[2 * a].astype(jnp.float32) * 512.0 + data[2 * a + 1].astype(jnp.float32))
        * (1.0 / LATTICE)
        for a in range(3)
    )
    c, s = cos_sin(x * first)
    c1, s1 = cos_sin(x)
    for i in range(4):
        put(2 * i, [c, s])
        if i < 3:
            c, s = c * c1 - s * s1, c * s1 + s * c1
    c1, s1 = cos_sin(y)
    c2, s2 = double(c1, s1)
    even = 1.0 - odd
    put(8, harmonics(odd * c1 + even * c2, odd * c1 + even, c2 + c2, 8))
    put(16, harmonics(odd * s1 + even * s2, -odd * s1, c2 + c2, 8))
    c1, s1 = cos_sin(z)
    put(24, harmonics(c1, jnp.ones_like(c1), c1 + c1, HALF))
    put(40, harmonics(s1, jnp.zeros_like(s1), c1 + c1, HALF))
    put(56, [data[6 + comp].astype(jnp.float32) for comp in range(3)])


def multiply(table, total):
    for pair in range(8):
        bases = [(2 * pair + k) * ROWS for k in range(2)]

        def rows(start, number):
            return [table[pl.ds(base + start, number), :] for base in bases]

        def wide(parts):
            return jnp.concatenate([p.astype(jnp.bfloat16) for p in parts], 1)

        yc, ys = rows(8, 8), rows(16, 8)
        left = []
        for i in range(4):
            cx, sx = rows(2 * i, 1), rows(2 * i + 1, 1)
            plus, minus = [], []
            for k in range(2):
                cc, sn = cx[k] * yc[k], sx[k] * ys[k]
                cn, sc = cx[k] * ys[k], sx[k] * yc[k]
                plus.append(jnp.concatenate([cc - sn, cn + sc], 0))
                minus.append(jnp.concatenate([cc + sn, sc - cn], 0))
            left += [wide(plus), wide(minus)]
        right = []
        for part in range(2):
            z = rows(24 + 16 * part, 16)
            right.append(wide(z))
            for comp in range(3):
                u = rows(56 + comp, 1)
                right.append(wide([z[k] * u[k] for k in range(2)]))
        total = total + lax.dot_general(
            jnp.concatenate(left, 0),
            jnp.concatenate(right, 0),
            (((1,), (1,)), ((), ())),
            preferred_element_type=jnp.float32,
        )
    return total


def modes_kernel(number, frames, more, last, waves, *refs):
    if more:
        before, refs = refs[0], refs[1:]
    data, out = refs[:number], refs[number]
    table_a, table_b, blocks, *rest = refs[number + 1 :]
    totals = rest[0] if last else out
    first, odd = waves[0], waves[1]
    steps = number * frames
    for g in range(number):
        for f in range(frames):
            blocks[f * number + g] = data[g][f]

    def block(index):
        return [blocks[index, k] for k in range(9)]

    totals[...] = before[...] if more else jnp.zeros_like(totals)
    fill(block(0), first, odd, table_a)

    def step(half, carry):
        now = 2 * half
        frame = now // number
        fill(block(now + 1), first, odd, table_b)
        total = multiply(table_a, totals[frame])
        fill(block(jnp.minimum(now + 2, steps - 1)), first, odd, table_a)
        totals[frame] = multiply(table_b, total)
        return carry

    lax.fori_loop(0, steps // 2, step, 0)
    if not last:
        return
    for f in range(frames):
        total = totals[f]
        for i in range(4):
            for b in range(4):
                minus, upper = b < 2, b in (0, 3)
                here = 32 * i + 16 * minus + 4 * upper
                there = 32 * (3 - i) + 16 * (not minus) + 4 * upper
                out[i * 4 + b, f] = jnp.concatenate(
                    [total[at + k : at + k + 4] for k in (0, 8) for at in (here, there)], 0
                )


def modes(waves, blocks, before=None, last=False):
    frames = blocks[0].shape[0]
    number, more = len(blocks), before is not None
    smem = pl.BlockSpec(memory_space=pltpu.SMEM)
    data = pl.BlockSpec((frames, 9, 16, 128), lambda _: (0, 0, 0, 0))
    sums = pl.BlockSpec((frames, 128, 128), lambda _: (0, 0, 0))
    owned = (16, frames, 16, 128)
    scratch = [
        pltpu.VMEM((16 * ROWS, 128), jnp.float32),
        pltpu.VMEM((16 * ROWS, 128), jnp.float32),
        pltpu.VMEM((number * frames, 9, 16, 128), jnp.bfloat16),
    ]
    work = number * frames * 2048
    return pl.pallas_call(
        functools.partial(modes_kernel, number, frames, more, last),
        grid=(1,),
        out_shape=jax.ShapeDtypeStruct(owned if last else (frames, 128, 128), jnp.float32),
        in_specs=[smem] + [sums] * more + [data] * number,
        out_specs=pl.BlockSpec(owned, lambda _: (0, 0, 0, 0)) if last else sums,
        scratch_shapes=scratch + [pltpu.VMEM((frames, 128, 128), jnp.float32)] * last,
        cost_estimate=pl.CostEstimate(
            flops=work * 128 * 128 * 2, bytes_accessed=work * 18, transcendentals=0
        ),
        name="last" if last else f"nearby{int(more)}",
    )(waves, *([before] * more), *blocks)


def correlate_kernel(flags, series, keep, send, d, e):
    frames = FRAMES
    d[frames:, :, :] = jnp.zeros((LAGS, 8, 128), jnp.float32)
    e[frames:, :, :] = jnp.zeros((LAGS, 8, 128), jnp.float32)

    def split(t, carry):
        values = series[t].astype(jnp.float32)
        real, imag = values[:8], pltpu.roll(values[8:], 64, 1)
        d[t] = real - imag
        e[t] = real + imag
        return carry

    lax.fori_loop(0, frames, split, 0, unroll=8)

    def lags(source):
        def step(t, sums):
            here = source[t]
            return tuple(sums[lag] + here * source[t + lag] for lag in range(LAGS))

        zero = jnp.zeros((8, 128), jnp.float32)
        return lax.fori_loop(0, frames, step, (zero,) * LAGS, unroll=4)

    sums_d, sums_e = lags(d), lags(e)
    mirrored = flags[1] == 1
    for lag in range(LAGS):
        value = (sums_d[lag] + pltpu.roll(sums_e[lag], 64, 1)) * (1.0 / (ATOMS * (frames - lag)))
        value = jnp.where(mirrored, pltpu.roll(value, 4, 0), value)
        keep[lag * 4 : lag * 4 + 4, :] = value[:4]
        send[lag * 4 : lag * 4 + 4, :] = value[4:]


def correlate(flags, series):
    vmem = pl.BlockSpec(memory_space=pltpu.VMEM)
    return pl.pallas_call(
        correlate_kernel,
        out_shape=[jax.ShapeDtypeStruct((4 * LAGS, 128), jnp.float32)] * 2,
        in_specs=[pl.BlockSpec(memory_space=pltpu.SMEM), vmem],
        out_specs=[vmem, vmem],
        scratch_shapes=[pltpu.VMEM((FRAMES + LAGS, 8, 128), jnp.float32)] * 2,
        name="correlate",
    )(flags, series)


def arrange_kernel(flags, keep, received, pick, out, rows):
    mirrored = flags[1] == 1
    kept, other = keep[...], received[...]
    rows[:64, :] = jnp.where(mirrored, other, kept)
    rows[64:, :] = jnp.where(mirrored, kept, other)
    rows[...] = jnp.dot(
        rows[...], pick[...], precision=lax.Precision.HIGHEST, preferred_element_type=jnp.float32
    )
    flip = flags[0] == 1
    lane = lax.broadcasted_iota(jnp.int32, (LAGS, 128), 1) // 32

    def wave(w):
        return rows[pl.ds(64 * (w % 2) + w // 2, LAGS, stride=4), :]

    for half in range(2):
        totals = [jnp.zeros((LAGS, 128), jnp.float32) for _ in range(4)]
        for part in range(4):
            w = half * 4 + part
            value = jnp.where(flip, wave(7 - w), wave(w))
            for comp in range(4):
                by = (32 * (part - comp)) % 128
                moved = pltpu.roll(value, by, 1) if by else value
                totals[comp] = jnp.where(lane == part, moved, totals[comp])
        for comp in range(4):
            out[comp, :, half * 128 : half * 128 + 128] = totals[comp]


def arrange(flags, keep, received):
    lane = jnp.arange(128)
    comp, q = lane // 32, lane % 32
    falling, rising = comp * 16 + 15 - q, comp * 16 + q - 16
    side = 64 * flags[1]
    source = jnp.where(q < 16, 64 - side + falling, side + rising)
    pick = (lane[:, None] == source[None, :]).astype(jnp.float32)
    vmem = pl.BlockSpec(memory_space=pltpu.VMEM)
    return pl.pallas_call(
        arrange_kernel,
        out_shape=jax.ShapeDtypeStruct((4, LAGS, 256), jnp.float32),
        in_specs=[pl.BlockSpec(memory_space=pltpu.SMEM), vmem, vmem, vmem],
        out_specs=vmem,
        scratch_shapes=[pltpu.VMEM((128, 128), jnp.float32)],
        name="arrange",
    )(flags, keep, received, pick)


def shift(block, by):
    return lax.ppermute(block, "atom", [(i, (i + by) % 8) for i in range(8)])


def swap(block):
    return lax.ppermute(block, "atom", [(i, i ^ 1) for i in range(8)])


def per_device(positions, velocity):
    a = lax.axis_index("atom")
    t = lax.axis_index("tm")
    frames = positions.shape[0]
    low = ((positions + 256) & 511) - 256
    high = (positions - low) >> 9
    parts = jnp.stack([high, low], 2).reshape(frames, 6, 16, 128).astype(jnp.bfloat16)
    own = jnp.concatenate([parts, velocity.reshape(frames, 3, 16, 128)], 1)
    positive = a >= 4
    first = 4 * jnp.maximum(a, 7 - a) - 15
    waves = jnp.stack([first, positive.astype(jnp.int32)]).astype(jnp.float32)
    left, right, across = shift(own, 2), shift(own, 6), shift(own, 4)
    sums = modes(waves, [own, swap(own)])
    left, right, sums = lax.optimization_barrier((left, right, sums))
    far = [swap(left), swap(right)]
    sums = modes(waves, [left, right], sums)
    across, sums, *far = lax.optimization_barrier((across, sums, *far))
    local = modes(waves, far + [across, swap(across)], sums, True)
    series = lax.all_to_all(local, "tm", split_axis=0, concat_axis=0, tiled=True)
    flags = jnp.stack([t % 4 < 2, ~positive]).astype(jnp.int32)
    keep, send = correlate(flags, series.reshape(FRAMES, 16, 128))
    received = lax.ppermute(send, "atom", [(i, 7 - i) for i in range(8)])
    return arrange(flags, keep, received)


def solution(mesh):
    in_specs = (P("tm", None, "atom"), P("tm", None, "atom"))
    out_specs = P(None, None, ("atom", "tm"))
    return jax.shard_map(
        per_device, mesh=mesh, in_specs=in_specs, out_specs=out_specs, check_vma=False
    )
```

```python
import functools
import math

import jax
import jax.numpy as jnp
from jax import lax
from jax.experimental import pallas as pl
from jax.experimental.pallas import tpu as pltpu
from jax.sharding import PartitionSpec as P

KX = 32
KY = 32
KZ = 32
LAGS = 16
LATTICE = 131072
ATOMS = 16384
FRAMES = 128
HALF = 16
LINK = jnp.bfloat16
ROWS = 59
SINE = (6.28318516, -41.3416550, 81.6010040, -76.5498338, 39.5367090)


def place():
    a, t = lax.axis_index("atom"), lax.axis_index("tm")
    return jnp.maximum(a, 7 - a), (a >= 4).astype(jnp.int32), t


def sine(u):
    square = u * u
    value = jnp.full_like(u, SINE[4])
    for factor in SINE[3::-1]:
        value = value * square + factor
    return value * u


def cos_sin(turns):
    r = turns - jnp.round(turns)
    c = sine(0.25 - jnp.abs(r))
    s = sine(jnp.maximum(jnp.minimum(r, 0.5 - r), -0.5 - r))
    return c, s


def double(c, s):
    return 2.0 * c * c - 1.0, 2.0 * s * c


def harmonics(here, before, twice, number):
    values = [here]
    for _ in range(number - 1):
        values.append(twice * values[-1] - before)
        before = values[-2]
    return values


def fill(data, first, odd, table):
    def put(row, values):
        for k, value in enumerate(values):
            table[pl.ds(row + k, 16, stride=ROWS), :] = value

    x, y, z = (
        (data[2 * a].astype(jnp.float32) * 512.0 + data[2 * a + 1].astype(jnp.float32))
        * (1.0 / LATTICE)
        for a in range(3)
    )
    c, s = cos_sin(x * first)
    c1, s1 = cos_sin(x)
    for i in range(4):
        put(2 * i, [c, s])
        if i < 3:
            c, s = c * c1 - s * s1, c * s1 + s * c1
    c1, s1 = cos_sin(y)
    c2, s2 = double(c1, s1)
    even = 1.0 - odd
    put(8, harmonics(odd * c1 + even * c2, odd * c1 + even, c2 + c2, 8))
    put(16, harmonics(odd * s1 + even * s2, -odd * s1, c2 + c2, 8))
    c1, s1 = cos_sin(z)
    put(24, harmonics(c1, jnp.ones_like(c1), c1 + c1, HALF))
    put(40, harmonics(s1, jnp.zeros_like(s1), c1 + c1, HALF))
    put(56, [data[6 + comp].astype(jnp.float32) for comp in range(3)])


def multiply(table, total):
    for pair in range(8):
        bases = [(2 * pair + k) * ROWS for k in range(2)]

        def rows(start, number):
            return [table[pl.ds(base + start, number), :] for base in bases]

        def wide(parts):
            return jnp.concatenate([p.astype(jnp.bfloat16) for p in parts], 1)

        yc, ys = rows(8, 8), rows(16, 8)
        left = []
        for i in range(4):
            cx, sx = rows(2 * i, 1), rows(2 * i + 1, 1)
            plus, minus = [], []
            for k in range(2):
                cc, sn = cx[k] * yc[k], sx[k] * ys[k]
                cn, sc = cx[k] * ys[k], sx[k] * yc[k]
                plus.append(jnp.concatenate([cc - sn, cn + sc], 0))
                minus.append(jnp.concatenate([cc + sn, sc - cn], 0))
            left += [wide(plus), wide(minus)]
        right = []
        for part in range(2):
            z = rows(24 + 16 * part, 16)
            right.append(wide(z))
            for comp in range(3):
                u = rows(56 + comp, 1)
                right.append(wide([z[k] * u[k] for k in range(2)]))
        total = total + lax.dot_general(
            jnp.concatenate(left, 0),
            jnp.concatenate(right, 0),
            (((1,), (1,)), ((), ())),
            preferred_element_type=jnp.float32,
        )
    return total


def modes_kernel(number, frames, more, last, *refs):
    if more:
        before, refs = refs[0], refs[1:]
    data, out = refs[:number], refs[number]
    table_a, table_b, blocks, *rest = refs[number + 1 :]
    totals = rest[0] if last else out
    pair, upper, _ = place()
    first, odd = (4 * pair - 15).astype(jnp.float32), upper.astype(jnp.float32)
    steps = number * frames
    for g in range(number):
        for f in range(frames):
            blocks[f * number + g] = data[g][f]

    def block(index):
        return [blocks[index, k] for k in range(9)]

    totals[...] = before[...] if more else jnp.zeros_like(totals)
    fill(block(0), first, odd, table_a)

    def step(half, carry):
        now = 2 * half
        frame = now // number
        fill(block(now + 1), first, odd, table_b)
        total = multiply(table_a, totals[frame])
        fill(block(jnp.minimum(now + 2, steps - 1)), first, odd, table_a)
        totals[frame] = multiply(table_b, total)
        return carry

    lax.fori_loop(0, steps // 2, step, 0)
    if not last:
        return
    for f in range(frames):
        total = totals[f].astype(LINK)
        for i in range(4):
            for b in range(4):
                minus, outer = b < 2, b in (0, 3)
                here = 32 * i + 16 * minus + 4 * outer
                there = 32 * (3 - i) + 16 * (not minus) + 4 * outer
                for side, at in enumerate((there, here)):
                    out[side * 16 + i * 4 + b, f] = jnp.concatenate(
                        [total[at : at + 4], total[at + 8 : at + 12]], 0
                    )


def modes(blocks, before=None, last=False):
    frames = blocks[0].shape[0]
    number, more = len(blocks), before is not None
    data = pl.BlockSpec((frames, 9, 16, 128), lambda _: (0, 0, 0, 0))
    sums = pl.BlockSpec((frames, 128, 128), lambda _: (0, 0, 0))
    owned = (32, frames, 8, 128)
    scratch = [
        pltpu.VMEM((16 * ROWS, 128), jnp.float32),
        pltpu.VMEM((16 * ROWS, 128), jnp.float32),
        pltpu.VMEM((number * frames, 9, 16, 128), jnp.bfloat16),
    ]
    work = number * frames * 2048
    return pl.pallas_call(
        functools.partial(modes_kernel, number, frames, more, last),
        grid=(1,),
        out_shape=jax.ShapeDtypeStruct(owned, LINK)
        if last
        else jax.ShapeDtypeStruct((frames, 128, 128), jnp.float32),
        in_specs=[sums] * more + [data] * number,
        out_specs=pl.BlockSpec(owned, lambda _: (0, 0, 0, 0)) if last else sums,
        scratch_shapes=scratch + [pltpu.VMEM((frames, 128, 128), jnp.float32)] * last,
        cost_estimate=pl.CostEstimate(
            flops=work * 128 * 128 * 2, bytes_accessed=work * 18, transcendentals=0
        ),
        name="last" if last else f"nearby{int(more)}",
    )(*([before] * more), *blocks)


def correlate_kernel(series, out, d, e, rows):
    frames = FRAMES
    d[frames:, :, :] = jnp.zeros((LAGS, 8, 128), jnp.float32)
    e[frames:, :, :] = jnp.zeros((LAGS, 8, 128), jnp.float32)
    lower = lax.broadcasted_iota(jnp.int32, (8, 128), 0) < 4

    def split(t, carry):
        even, odd = (series[side, t].astype(jnp.float32) for side in range(2))
        real = jnp.where(lower, odd, pltpu.roll(even, 4, 0))
        imag = pltpu.roll(jnp.where(lower, pltpu.roll(odd, 4, 0), even), 64, 1)
        d[t] = real - imag
        e[t] = real + imag
        return carry

    lax.fori_loop(0, frames, split, 0, unroll=8)

    def lags(source):
        def step(t, sums):
            here = source[t]
            return tuple(sums[lag] + here * source[t + lag] for lag in range(LAGS))

        zero = jnp.zeros((8, 128), jnp.float32)
        return lax.fori_loop(0, frames, step, (zero,) * LAGS, unroll=4)

    sums_d, sums_e = lags(d), lags(e)
    for lag in range(LAGS):
        value = (sums_d[lag] + pltpu.roll(sums_e[lag], 64, 1)) * (1.0 / (ATOMS * (frames - lag)))
        rows[lag * 8 : lag * 8 + 8, :] = value

    _, upper, t = place()
    lane = lax.broadcasted_iota(jnp.int32, (128, 128), 1)
    comp, q = (lane // 32) * 16, lane % 32
    falling, rising = comp + 15 - q, comp + q - 16
    source = jnp.where(q < 16, 64 * upper + falling, 64 * (1 - upper) + rising)
    pick = (lax.broadcasted_iota(jnp.int32, (128, 128), 0) == source).astype(jnp.float32)
    rows[...] = jnp.dot(
        rows[...], pick, precision=lax.Precision.HIGHEST, preferred_element_type=jnp.float32
    )
    flip = t % 4 < 2
    group = lax.broadcasted_iota(jnp.int32, (LAGS, 128), 1) // 32

    def wave(w):
        return rows[pl.ds(4 * (w % 2) + w // 2, LAGS, stride=8), :]

    for half in range(2):
        totals = [jnp.zeros((LAGS, 128), jnp.float32) for _ in range(4)]
        for part in range(4):
            w = half * 4 + part
            value = jnp.where(flip, wave(7 - w), wave(w))
            for comp in range(4):
                by = (32 * (part - comp)) % 128
                moved = pltpu.roll(value, by, 1) if by else value
                totals[comp] = jnp.where(group == part, moved, totals[comp])
        for comp in range(4):
            out[comp, :, half * 128 : half * 128 + 128] = totals[comp]


def correlate(series):
    vmem = pl.BlockSpec(memory_space=pltpu.VMEM)
    return pl.pallas_call(
        correlate_kernel,
        out_shape=jax.ShapeDtypeStruct((4, LAGS, 256), jnp.float32),
        in_specs=[vmem],
        out_specs=vmem,
        scratch_shapes=[
            pltpu.VMEM((FRAMES + LAGS, 8, 128), jnp.float32),
            pltpu.VMEM((FRAMES + LAGS, 8, 128), jnp.float32),
            pltpu.VMEM((128, 128), jnp.float32),
        ],
        name="correlate",
    )(series)


def shift(block, by):
    return lax.ppermute(block, "atom", [(i, (i + by) % 8) for i in range(8)])


def swap(block):
    return lax.ppermute(block, "atom", [(i, i ^ 1) for i in range(8)])


def exchange(local):
    groups = [[a * 16 + t for a in (lower, 7 - lower) for t in range(16)] for lower in range(4)]
    series = lax.all_to_all(
        local, ("atom", "tm"), 0, 0, tiled=True, axis_index_groups=groups
    )
    return series.reshape(2, FRAMES, 8, 128)


def per_device(positions, velocity):
    frames = positions.shape[0]
    low = ((positions + 256) & 511) - 256
    high = (positions - low) >> 9
    parts = jnp.stack([high, low], 2).reshape(frames, 6, 16, 128).astype(jnp.bfloat16)
    own = jnp.concatenate([parts, velocity.reshape(frames, 3, 16, 128)], 1)
    left, right, across = shift(own, 2), shift(own, 6), shift(own, 4)
    sums = modes([own, swap(own)])
    left, right, sums = lax.optimization_barrier((left, right, sums))
    far = [swap(left), swap(right)]
    sums = modes([left, right], sums)
    across, sums, *far = lax.optimization_barrier((across, sums, *far))
    return correlate(exchange(modes(far + [across, swap(across)], sums, True)))


def solution(mesh):
    in_specs = (P("tm", None, "atom"), P("tm", None, "atom"))
    out_specs = P(None, None, ("atom", "tm"))
    return jax.shard_map(
        per_device, mesh=mesh, in_specs=in_specs, out_specs=out_specs, check_vma=False
    )
```

```python
import functools
import math

import jax
import jax.numpy as jnp
from jax import lax
from jax.experimental import pallas as pl
from jax.experimental.pallas import tpu as pltpu
from jax.sharding import PartitionSpec as P

KX = 32
KY = 32
KZ = 32
LAGS = 16
LATTICE = 131072
ATOMS = 16384
FRAMES = 128
HALF = 16
LINK = jnp.bfloat16
ROWS = 75
SINE = (6.28318516, -41.3416550, 81.6010040, -76.5498338, 39.5367090)


def place():
    a, t = lax.axis_index("atom"), lax.axis_index("tm")
    return jnp.maximum(a, 7 - a), (a >= 4).astype(jnp.int32), t


def sine(u):
    square = u * u
    value = jnp.full_like(u, SINE[4])
    for factor in SINE[3::-1]:
        value = value * square + factor
    return value * u


def cos_sin(turns):
    r = turns - jnp.round(turns)
    c = sine(0.25 - jnp.abs(r))
    s = sine(jnp.maximum(jnp.minimum(r, 0.5 - r), -0.5 - r))
    return c, s


def harmonics(here, before, twice, number):
    values = [here]
    for _ in range(number - 1):
        values.append(twice * values[-1] - before)
        before = values[-2]
    return values


def fill(data, first, table):
    def put(row, values):
        for k, value in enumerate(values):
            table[pl.ds(row + k, 16, stride=ROWS), :] = value

    x, y, z = (
        (data[2 * a].astype(jnp.float32) * 512.0 + data[2 * a + 1].astype(jnp.float32))
        * (1.0 / LATTICE)
        for a in range(3)
    )
    c, s = cos_sin(x * first)
    c1, s1 = cos_sin(x)
    for i in range(4):
        put(2 * i, [c, s])
        if i < 3:
            c, s = c * c1 - s * s1, c * s1 + s * c1
    for row, angle in ((8, y), (40, z)):
        c1, s1 = cos_sin(angle)
        put(row, harmonics(c1, jnp.ones_like(c1), c1 + c1, HALF))
        put(row + HALF, harmonics(s1, jnp.zeros_like(s1), c1 + c1, HALF))
    put(72, [data[6 + comp].astype(jnp.float32) for comp in range(3)])


def multiply(table, total):
    for pair in range(8):
        bases = [(2 * pair + k) * ROWS for k in range(2)]

        def rows(start, number):
            return [table[pl.ds(base + start, number), :] for base in bases]

        def wide(parts):
            return jnp.concatenate([p.astype(jnp.bfloat16) for p in parts], 1)

        yc = [rows(8 + 8 * b, 8) for b in range(2)]
        ys = [rows(24 + 8 * b, 8) for b in range(2)]
        left = []
        for i in range(4):
            cx, sx = rows(2 * i, 1), rows(2 * i + 1, 1)
            for b in range(2):
                plus, minus = [], []
                for k in range(2):
                    cc, sn = cx[k] * yc[b][k], sx[k] * ys[b][k]
                    cn, sc = cx[k] * ys[b][k], sx[k] * yc[b][k]
                    plus.append(jnp.concatenate([cc - sn, cn + sc], 0))
                    minus.append(jnp.concatenate([cc + sn, sc - cn], 0))
                left += [wide(plus), wide(minus)]
        right = []
        for part in range(2):
            z = rows(40 + 16 * part, 16)
            right.append(wide(z))
            for comp in range(3):
                u = rows(72 + comp, 1)
                right.append(wide([z[k] * u[k] for k in range(2)]))
        total = total + lax.dot_general(
            jnp.concatenate(left, 0),
            jnp.concatenate(right, 0),
            (((1,), (1,)), ((), ())),
            preferred_element_type=jnp.float32,
        )
    return total


def modes_kernel(number, frames, more, last, *refs):
    if more:
        before, refs = refs[0], refs[1:]
    data, out = refs[:number], refs[number]
    table_a, table_b, blocks, *rest = refs[number + 1 :]
    totals = rest[0] if last else out
    first = (4 * place()[0] - 15).astype(jnp.float32)
    steps = number * frames
    for g in range(number):
        for f in range(frames):
            blocks[f * number + g] = data[g][f]

    def block(index):
        return [blocks[index, k] for k in range(9)]

    totals[...] = before[...] if more else jnp.zeros_like(totals)
    fill(block(0), first, table_a)

    def step(half, carry):
        now = 2 * half
        frame = now // number
        fill(block(now + 1), first, table_b)
        total = multiply(table_a, totals[frame])
        fill(block(jnp.minimum(now + 2, steps - 1)), first, table_a)
        totals[frame] = multiply(table_b, total)
        return carry

    lax.fori_loop(0, steps // 2, step, 0)
    if not last:
        return
    for f in range(frames):
        total = totals[f].astype(LINK)
        for i in range(4):
            for b in range(4):
                minus, outer = b < 2, b in (0, 3)
                here = 64 * i + 32 * outer + 16 * minus
                there = 64 * (3 - i) + 32 * outer + 16 * (not minus)
                out[i * 4 + b, f] = total[there : there + 16]
                out[16 + i * 4 + b, f] = total[here : here + 16]


def modes(blocks, before=None, last=False):
    frames = blocks[0].shape[0]
    number, more = len(blocks), before is not None
    data = pl.BlockSpec((frames, 9, 16, 128), lambda _: (0, 0, 0, 0))
    sums = pl.BlockSpec((frames, 256, 128), lambda _: (0, 0, 0))
    owned = (32, frames, 16, 128)
    scratch = [
        pltpu.VMEM((16 * ROWS, 128), jnp.float32),
        pltpu.VMEM((16 * ROWS, 128), jnp.float32),
        pltpu.VMEM((number * frames, 9, 16, 128), jnp.bfloat16),
    ]
    work = number * frames * 2048
    return pl.pallas_call(
        functools.partial(modes_kernel, number, frames, more, last),
        grid=(1,),
        out_shape=jax.ShapeDtypeStruct(owned, LINK)
        if last
        else jax.ShapeDtypeStruct((frames, 256, 128), jnp.float32),
        in_specs=[sums] * more + [data] * number,
        out_specs=pl.BlockSpec(owned, lambda _: (0, 0, 0, 0)) if last else sums,
        scratch_shapes=scratch + [pltpu.VMEM((frames, 256, 128), jnp.float32)] * last,
        cost_estimate=pl.CostEstimate(
            flops=work * 256 * 128 * 2, bytes_accessed=work * 18, transcendentals=0
        ),
        name="last" if last else f"nearby{int(more)}",
    )(*([before] * more), *blocks)


def correlate_kernel(series, out, d, e, rows):
    frames = FRAMES
    d[frames:, :, :] = jnp.zeros((LAGS, 8, 128), jnp.float32)
    e[frames:, :, :] = jnp.zeros((LAGS, 8, 128), jnp.float32)

    def split(t, carry):
        values = series[0, t].astype(jnp.float32) + series[1, t].astype(jnp.float32)
        real, imag = values[:8], pltpu.roll(values[8:], 64, 1)
        d[t] = real - imag
        e[t] = real + imag
        return carry

    lax.fori_loop(0, frames, split, 0, unroll=8)

    def lags(source):
        def step(t, sums):
            here = source[t]
            return tuple(sums[lag] + here * source[t + lag] for lag in range(LAGS))

        zero = jnp.zeros((8, 128), jnp.float32)
        return lax.fori_loop(0, frames, step, (zero,) * LAGS, unroll=4)

    sums_d, sums_e = lags(d), lags(e)
    for lag in range(LAGS):
        value = (sums_d[lag] + pltpu.roll(sums_e[lag], 64, 1)) * (1.0 / (ATOMS * (frames - lag)))
        rows[lag * 8 : lag * 8 + 8, :] = value

    _, upper, t = place()
    lane = lax.broadcasted_iota(jnp.int32, (128, 128), 1)
    comp, q = (lane // 32) * 16, lane % 32
    falling, rising = comp + 15 - q, comp + q - 16
    source = jnp.where(q < 16, 64 * upper + falling, 64 * (1 - upper) + rising)
    pick = (lax.broadcasted_iota(jnp.int32, (128, 128), 0) == source).astype(jnp.float32)
    rows[...] = jnp.dot(
        rows[...], pick, precision=lax.Precision.HIGHEST, preferred_element_type=jnp.float32
    )
    flip = t % 4 < 2
    group = lax.broadcasted_iota(jnp.int32, (LAGS, 128), 1) // 32

    def wave(w):
        return rows[pl.ds(w, LAGS, stride=8), :]

    for half in range(2):
        totals = [jnp.zeros((LAGS, 128), jnp.float32) for _ in range(4)]
        for part in range(4):
            w = half * 4 + part
            value = jnp.where(flip, wave(7 - w), wave(w))
            for comp in range(4):
                by = (32 * (part - comp)) % 128
                moved = pltpu.roll(value, by, 1) if by else value
                totals[comp] = jnp.where(group == part, moved, totals[comp])
        for comp in range(4):
            out[comp, :, half * 128 : half * 128 + 128] = totals[comp]


def correlate(series):
    vmem = pl.BlockSpec(memory_space=pltpu.VMEM)
    return pl.pallas_call(
        correlate_kernel,
        out_shape=jax.ShapeDtypeStruct((4, LAGS, 256), jnp.float32),
        in_specs=[vmem],
        out_specs=vmem,
        scratch_shapes=[
            pltpu.VMEM((FRAMES + LAGS, 8, 128), jnp.float32),
            pltpu.VMEM((FRAMES + LAGS, 8, 128), jnp.float32),
            pltpu.VMEM((128, 128), jnp.float32),
        ],
        name="correlate",
    )(series)


def across(block):
    return lax.ppermute(block, "atom", [(i, i ^ 2) for i in range(8)])


def swap(block):
    return lax.ppermute(block, "atom", [(i, i ^ 1) for i in range(8)])


def exchange(local):
    groups = [[a * 16 + t for a in (lower, 7 - lower) for t in range(16)] for lower in range(4)]
    series = lax.all_to_all(
        local, ("atom", "tm"), 0, 0, tiled=True, axis_index_groups=groups
    )
    return series.reshape(2, FRAMES, 16, 128)


def per_device(positions, velocity):
    frames = positions.shape[0]
    low = ((positions + 256) & 511) - 256
    high = (positions - low) >> 9
    parts = jnp.stack([high, low], 2).reshape(frames, 6, 16, 128).astype(jnp.bfloat16)
    own = jnp.concatenate([parts, velocity.reshape(frames, 3, 16, 128)], 1)
    other = across(own)
    sums = modes([own, swap(own)])
    other, sums = lax.optimization_barrier((other, sums))
    return correlate(exchange(modes([other, swap(other)], sums, True)))


def solution(mesh):
    in_specs = (P("tm", None, "atom"), P("tm", None, "atom"))
    out_specs = P(None, None, ("atom", "tm"))
    return jax.shard_map(
        per_device, mesh=mesh, in_specs=in_specs, out_specs=out_specs, check_vma=False
    )
```

```python
import functools
import math

import jax
import jax.numpy as jnp
from jax import lax
from jax.experimental import pallas as pl
from jax.experimental.pallas import tpu as pltpu
from jax.sharding import PartitionSpec as P

KX = 32
KY = 32
KZ = 32
LAGS = 16
LATTICE = 131072
ATOMS = 16384
FRAMES = 128
HALF = 16
LINK = jnp.bfloat16
WIDTH = 2
GRANT = 16 << 20
ROWS = 75
SINE = (6.28318516, -41.3416550, 81.6010040, -76.5498338, 39.5367090)


def place():
    a, t = lax.axis_index("atom"), lax.axis_index("tm")
    return jnp.maximum(a, 7 - a), (a >= 4).astype(jnp.int32), t


def sine(u):
    square = u * u
    value = jnp.full_like(u, SINE[4])
    for factor in SINE[3::-1]:
        value = value * square + factor
    return value * u


def cos_sin(turns):
    r = turns - jnp.round(turns)
    c = sine(0.25 - jnp.abs(r))
    s = sine(jnp.maximum(jnp.minimum(r, 0.5 - r), -0.5 - r))
    return c, s


def harmonics(here, before, twice, number):
    values = [here]
    for _ in range(number - 1):
        values.append(twice * values[-1] - before)
        before = values[-2]
    return values


def fill(data, first, table):
    def put(row, values):
        for k, value in enumerate(values):
            table[pl.ds(row + k, 16, stride=ROWS), :] = value

    x, y, z = (
        (data[2 * a].astype(jnp.float32) * 512.0 + data[2 * a + 1].astype(jnp.float32))
        * (1.0 / LATTICE)
        for a in range(3)
    )
    c, s = cos_sin(x * first)
    c1, s1 = cos_sin(x)
    for i in range(4):
        put(2 * i, [c, s])
        if i < 3:
            c, s = c * c1 - s * s1, c * s1 + s * c1
    for row, angle in ((8, y), (40, z)):
        c1, s1 = cos_sin(angle)
        put(row, harmonics(c1, jnp.ones_like(c1), c1 + c1, HALF))
        put(row + HALF, harmonics(s1, jnp.zeros_like(s1), c1 + c1, HALF))
    put(72, [data[6 + comp].astype(jnp.float32) for comp in range(3)])


def multiply(table, total):
    for start in range(0, 16, WIDTH):
        bases = [(start + k) * ROWS for k in range(WIDTH)]

        def rows(start, number):
            return [table[pl.ds(base + start, number), :] for base in bases]

        def wide(parts):
            return jnp.concatenate([p.astype(jnp.bfloat16) for p in parts], 1)

        yc = [rows(8 + 8 * b, 8) for b in range(2)]
        ys = [rows(24 + 8 * b, 8) for b in range(2)]
        left = []
        for i in range(4):
            cx, sx = rows(2 * i, 1), rows(2 * i + 1, 1)
            for b in range(2):
                plus, minus = [], []
                for k in range(WIDTH):
                    cc, sn = cx[k] * yc[b][k], sx[k] * ys[b][k]
                    cn, sc = cx[k] * ys[b][k], sx[k] * yc[b][k]
                    plus.append(jnp.concatenate([cc - sn, cn + sc], 0))
                    minus.append(jnp.concatenate([cc + sn, sc - cn], 0))
                left += [wide(plus), wide(minus)]
        right = []
        for part in range(2):
            z = rows(40 + 16 * part, 16)
            right.append(wide(z))
            for comp in range(3):
                u = rows(72 + comp, 1)
                right.append(wide([z[k] * u[k] for k in range(WIDTH)]))
        total = total + lax.dot_general(
            jnp.concatenate(left, 0),
            jnp.concatenate(right, 0),
            (((1,), (1,)), ((), ())),
            preferred_element_type=jnp.float32,
        )
    return total


def modes_kernel(number, frames, more, last, *refs):
    data, refs = refs[:number], refs[number:]
    if more:
        before, refs = refs[0], refs[1:]
    out, table_a, table_b, blocks, *rest = refs
    totals = rest[0] if last else out
    first = (4 * place()[0] - 15).astype(jnp.float32)
    steps = number * frames
    for g in range(number):
        for f in range(frames):
            blocks[g * frames + f] = data[g][f]

    def block(index):
        return [blocks[index, k] for k in range(9)]

    totals[...] = before[...] if more else jnp.zeros_like(totals)
    fill(block(0), first, table_a)

    def step(half, carry):
        now = 2 * half
        frame = now % frames
        fill(block(now + 1), first, table_b)
        totals[frame] = multiply(table_a, totals[frame])
        fill(block(jnp.minimum(now + 2, steps - 1)), first, table_a)
        totals[frame + 1] = multiply(table_b, totals[frame + 1])
        return carry

    lax.fori_loop(0, steps // 2, step, 0)
    if not last:
        return
    for f in range(frames):
        total = totals[f].astype(LINK)
        for i in range(4):
            for b in range(4):
                minus, outer = b < 2, b in (0, 3)
                here = 64 * i + 32 * outer + 16 * minus
                there = 64 * (3 - i) + 32 * outer + 16 * (not minus)
                out[i * 4 + b, f] = total[there : there + 16]
                out[16 + i * 4 + b, f] = total[here : here + 16]


def modes(blocks, before=None, last=False):
    frames = blocks[0].shape[0]
    number, more = len(blocks), before is not None
    vmem = pl.BlockSpec(memory_space=pltpu.VMEM)
    sums = (frames, 256, 128)
    work = number * frames * 2048
    return pl.pallas_call(
        functools.partial(modes_kernel, number, frames, more, last),
        out_shape=jax.ShapeDtypeStruct((32, frames, 16, 128), LINK)
        if last
        else jax.ShapeDtypeStruct(sums, jnp.float32),
        in_specs=[vmem] * (number + more),
        out_specs=vmem,
        scratch_shapes=[
            pltpu.VMEM((16 * ROWS, 128), jnp.float32),
            pltpu.VMEM((16 * ROWS, 128), jnp.float32),
            pltpu.VMEM((number * frames, 9, 16, 128), jnp.bfloat16),
        ]
        + [pltpu.VMEM(sums, jnp.float32)] * last,
        input_output_aliases={number: 0} if more and not last else {},
        cost_estimate=pl.CostEstimate(
            flops=work * 256 * 128 * 2, bytes_accessed=work * 18, transcendentals=0
        ),
        compiler_params=pltpu.CompilerParams(vmem_limit_bytes=GRANT),
        name="last" if last else f"nearby{int(more)}",
    )(*blocks, *([before] * more))


def correlate_kernel(series, out, d, e, rows):
    frames = FRAMES
    d[frames:, :, :] = jnp.zeros((LAGS, 8, 128), jnp.float32)
    e[frames:, :, :] = jnp.zeros((LAGS, 8, 128), jnp.float32)

    def split(t, carry):
        values = series[0, t].astype(jnp.float32) + series[1, t].astype(jnp.float32)
        real, imag = values[:8], pltpu.roll(values[8:], 64, 1)
        d[t] = real - imag
        e[t] = real + imag
        return carry

    lax.fori_loop(0, frames, split, 0, unroll=8)

    def lags(source):
        def step(t, sums):
            here = source[t]
            return tuple(sums[lag] + here * source[t + lag] for lag in range(LAGS))

        zero = jnp.zeros((8, 128), jnp.float32)
        return lax.fori_loop(0, frames, step, (zero,) * LAGS, unroll=4)

    sums_d, sums_e = lags(d), lags(e)
    for lag in range(LAGS):
        value = (sums_d[lag] + pltpu.roll(sums_e[lag], 64, 1)) * (1.0 / (ATOMS * (frames - lag)))
        rows[lag * 8 : lag * 8 + 8, :] = value

    _, upper, t = place()
    lane = lax.broadcasted_iota(jnp.int32, (128, 128), 1)
    comp, q = (lane // 32) * 16, lane % 32
    falling, rising = comp + 15 - q, comp + q - 16
    source = jnp.where(q < 16, 64 * upper + falling, 64 * (1 - upper) + rising)
    pick = (lax.broadcasted_iota(jnp.int32, (128, 128), 0) == source).astype(jnp.float32)
    rows[...] = jnp.dot(
        rows[...], pick, precision=lax.Precision.HIGHEST, preferred_element_type=jnp.float32
    )
    flip = t % 4 < 2
    group = lax.broadcasted_iota(jnp.int32, (LAGS, 128), 1) // 32

    def wave(w):
        return rows[pl.ds(w, LAGS, stride=8), :]

    for half in range(2):
        totals = [jnp.zeros((LAGS, 128), jnp.float32) for _ in range(4)]
        for part in range(4):
            w = half * 4 + part
            value = jnp.where(flip, wave(7 - w), wave(w))
            for comp in range(4):
                by = (32 * (part - comp)) % 128
                moved = pltpu.roll(value, by, 1) if by else value
                totals[comp] = jnp.where(group == part, moved, totals[comp])
        for comp in range(4):
            out[comp, :, half * 128 : half * 128 + 128] = totals[comp]


def correlate(series):
    vmem = pl.BlockSpec(memory_space=pltpu.VMEM)
    return pl.pallas_call(
        correlate_kernel,
        out_shape=jax.ShapeDtypeStruct((4, LAGS, 256), jnp.float32),
        in_specs=[vmem],
        out_specs=vmem,
        scratch_shapes=[
            pltpu.VMEM((FRAMES + LAGS, 8, 128), jnp.float32),
            pltpu.VMEM((FRAMES + LAGS, 8, 128), jnp.float32),
            pltpu.VMEM((128, 128), jnp.float32),
        ],
        compiler_params=pltpu.CompilerParams(vmem_limit_bytes=GRANT),
        name="correlate",
    )(series)


def across(block):
    return lax.ppermute(block, "atom", [(i, i ^ 2) for i in range(8)])


def swap(block):
    return lax.ppermute(block, "atom", [(i, i ^ 1) for i in range(8)])


def exchange(local):
    groups = [[a * 16 + t for a in (lower, 7 - lower) for t in range(16)] for lower in range(4)]
    series = lax.all_to_all(
        local, ("atom", "tm"), 0, 0, tiled=True, axis_index_groups=groups
    )
    return series.reshape(2, FRAMES, 16, 128)


def per_device(positions, velocity):
    frames = positions.shape[0]
    low = ((positions + 256) & 511) - 256
    high = (positions - low) >> 9
    parts = jnp.stack([high, low], 2).reshape(frames, 6, 16, 128).astype(jnp.bfloat16)
    own = jnp.concatenate([parts, velocity.reshape(frames, 3, 16, 128)], 1)
    other = across(own)
    sums = modes([own, swap(own)])
    other, sums = lax.optimization_barrier((other, sums))
    behind = swap(other)
    sums = modes([other], sums)
    return correlate(exchange(modes([behind], sums, True)))


def solution(mesh):
    in_specs = (P("tm", None, "atom"), P("tm", None, "atom"))
    out_specs = P(None, None, ("atom", "tm"))
    return jax.shard_map(
        per_device, mesh=mesh, in_specs=in_specs, out_specs=out_specs, check_vma=False
    )
```

```python
import functools
import math

import jax
import jax.numpy as jnp
from jax import lax
from jax.experimental import pallas as pl
from jax.experimental.pallas import tpu as pltpu
from jax.sharding import PartitionSpec as P

KX = 32
KY = 32
KZ = 32
LAGS = 16
LATTICE = 131072
ATOMS = 16384
FRAMES = 128
HALF = 16
LINK = jnp.bfloat16
WIDTH = 2
SPREAD = 136
GRANT = 16 << 20
ROWS = 75
SINE = (6.28318516, -41.3416550, 81.6010040, -76.5498338, 39.5367090)


def place():
    a, t = lax.axis_index("atom"), lax.axis_index("tm")
    return jnp.maximum(a, 7 - a), (a >= 4).astype(jnp.int32), t


def sine(u):
    square = u * u
    value = jnp.full_like(u, SINE[4])
    for factor in SINE[3::-1]:
        value = value * square + factor
    return value * u


def cos_sin(turns):
    r = turns - jnp.round(turns)
    c = sine(0.25 - jnp.abs(r))
    s = sine(jnp.maximum(jnp.minimum(r, 0.5 - r), -0.5 - r))
    return c, s


def harmonics(here, before, twice, number):
    values = [here]
    for _ in range(number - 1):
        values.append(twice * values[-1] - before)
        before = values[-2]
    return values


def fill(data, first, table):
    def put(row, values):
        for k, value in enumerate(values):
            table[pl.ds(row + k, 16, stride=ROWS), :] = value

    x, y, z = (
        (data[2 * a].astype(jnp.float32) * 512.0 + data[2 * a + 1].astype(jnp.float32))
        * (1.0 / LATTICE)
        for a in range(3)
    )
    c, s = cos_sin(x * first)
    c1, s1 = cos_sin(x)
    for i in range(4):
        put(2 * i, [c, s])
        if i < 3:
            c, s = c * c1 - s * s1, c * s1 + s * c1
    for row, angle in ((8, y), (40, z)):
        c1, s1 = cos_sin(angle)
        put(row, harmonics(c1, jnp.ones_like(c1), c1 + c1, HALF))
        put(row + HALF, harmonics(s1, jnp.zeros_like(s1), c1 + c1, HALF))
    put(72, [data[6 + comp].astype(jnp.float32) for comp in range(3)])


def prepare_kernel(far_positions, far_velocity, out, positions, velocity, spread, sem):
    frames = positions.shape[1]
    copies = [
        pltpu.make_async_copy(far_positions, positions, sem.at[0]),
        pltpu.make_async_copy(far_velocity, velocity, sem.at[1]),
    ]
    for copy in copies:
        copy.start()
    for copy in copies:
        copy.wait()
    for g in range(16):
        lanes = slice(g * 128, (g + 1) * 128)
        for a in range(3):
            whole = positions[a, :, lanes]
            low = ((whole + 256) & 511) - 256
            high = (whole - low) >> 9
            parts = (high, low, velocity[a, :, lanes])
            for k, part in zip((2 * a, 2 * a + 1, 6 + a), parts):
                spread[pl.ds(k * SPREAD + g, frames, stride=17), :] = part.astype(jnp.float32)
    for f in range(frames):
        for k in range(9):
            at = k * SPREAD + 17 * f
            out[f, k] = spread[at : at + 16, :].astype(jnp.bfloat16)


def prepare(positions, velocity):
    frames = positions.shape[0]
    vmem = pl.BlockSpec(memory_space=pltpu.VMEM)
    return pl.pallas_call(
        prepare_kernel,
        out_shape=jax.ShapeDtypeStruct((frames, 9, 16, 128), jnp.bfloat16),
        in_specs=[pl.BlockSpec(memory_space=pltpu.HBM)] * 2,
        out_specs=vmem,
        scratch_shapes=[
            pltpu.VMEM((3, frames, 2048), jnp.int32),
            pltpu.VMEM((3, frames, 2048), jnp.bfloat16),
            pltpu.VMEM((9 * SPREAD, 128), jnp.float32),
            pltpu.SemaphoreType.DMA((2,)),
        ],
        compiler_params=pltpu.CompilerParams(vmem_limit_bytes=GRANT),
        name="prepare",
    )(
        *(
            pltpu.with_memory_space_constraint(jnp.transpose(x, (1, 0, 2)), pltpu.HBM)
            for x in (positions, velocity)
        )
    )


def multiply(table, total):
    for start in range(0, 16, WIDTH):
        bases = [(start + k) * ROWS for k in range(WIDTH)]

        def rows(start, number):
            return [table[pl.ds(base + start, number), :] for base in bases]

        def wide(parts):
            return jnp.concatenate([p.astype(jnp.bfloat16) for p in parts], 1)

        yc = [rows(8 + 8 * b, 8) for b in range(2)]
        ys = [rows(24 + 8 * b, 8) for b in range(2)]
        left = []
        for i in range(4):
            cx, sx = rows(2 * i, 1), rows(2 * i + 1, 1)
            for b in range(2):
                plus, minus = [], []
                for k in range(WIDTH):
                    cc, sn = cx[k] * yc[b][k], sx[k] * ys[b][k]
                    cn, sc = cx[k] * ys[b][k], sx[k] * yc[b][k]
                    plus.append(jnp.concatenate([cc - sn, cn + sc], 0))
                    minus.append(jnp.concatenate([cc + sn, sc - cn], 0))
                left += [wide(plus), wide(minus)]
        right = []
        for part in range(2):
            z = rows(40 + 16 * part, 16)
            right.append(wide(z))
            for comp in range(3):
                u = rows(72 + comp, 1)
                right.append(wide([z[k] * u[k] for k in range(WIDTH)]))
        total = total + lax.dot_general(
            jnp.concatenate(left, 0),
            jnp.concatenate(right, 0),
            (((1,), (1,)), ((), ())),
            preferred_element_type=jnp.float32,
        )
    return total


def modes_kernel(number, frames, more, last, *refs):
    data, refs = refs[:number], refs[number:]
    if more:
        before, refs = refs[0], refs[1:]
    out, table_a, table_b, blocks, *rest = refs
    totals = rest[0] if last else out
    first = (4 * place()[0] - 15).astype(jnp.float32)
    steps = number * frames
    for g in range(number):
        for f in range(frames):
            blocks[g * frames + f] = data[g][f]

    def block(index):
        return [blocks[index, k] for k in range(9)]

    totals[...] = before[...] if more else jnp.zeros_like(totals)
    fill(block(0), first, table_a)

    def step(half, carry):
        now = 2 * half
        frame = now % frames
        fill(block(now + 1), first, table_b)
        totals[frame] = multiply(table_a, totals[frame])
        fill(block(jnp.minimum(now + 2, steps - 1)), first, table_a)
        totals[frame + 1] = multiply(table_b, totals[frame + 1])
        return carry

    lax.fori_loop(0, steps // 2, step, 0)
    if not last:
        return
    for f in range(frames):
        total = totals[f].astype(LINK)
        for i in range(4):
            for b in range(4):
                minus, outer = b < 2, b in (0, 3)
                here = 64 * i + 32 * outer + 16 * minus
                there = 64 * (3 - i) + 32 * outer + 16 * (not minus)
                out[i * 4 + b, f] = total[there : there + 16]
                out[16 + i * 4 + b, f] = total[here : here + 16]


def modes(blocks, before=None, last=False):
    frames = blocks[0].shape[0]
    number, more = len(blocks), before is not None
    vmem = pl.BlockSpec(memory_space=pltpu.VMEM)
    sums = (frames, 256, 128)
    work = number * frames * 2048
    return pl.pallas_call(
        functools.partial(modes_kernel, number, frames, more, last),
        out_shape=jax.ShapeDtypeStruct((32, frames, 16, 128), LINK)
        if last
        else jax.ShapeDtypeStruct(sums, jnp.float32),
        in_specs=[vmem] * (number + more),
        out_specs=vmem,
        scratch_shapes=[
            pltpu.VMEM((16 * ROWS, 128), jnp.float32),
            pltpu.VMEM((16 * ROWS, 128), jnp.float32),
            pltpu.VMEM((number * frames, 9, 16, 128), jnp.bfloat16),
        ]
        + [pltpu.VMEM(sums, jnp.float32)] * last,
        input_output_aliases={number: 0} if more and not last else {},
        cost_estimate=pl.CostEstimate(
            flops=work * 256 * 128 * 2, bytes_accessed=work * 18, transcendentals=0
        ),
        compiler_params=pltpu.CompilerParams(vmem_limit_bytes=GRANT),
        name="last" if last else f"nearby{int(more)}",
    )(*blocks, *([before] * more))


def correlate_kernel(series, out, d, e, rows):
    frames = FRAMES
    d[frames:, :, :] = jnp.zeros((LAGS, 8, 128), jnp.float32)
    e[frames:, :, :] = jnp.zeros((LAGS, 8, 128), jnp.float32)

    def split(t, carry):
        values = series[0, t].astype(jnp.float32) + series[1, t].astype(jnp.float32)
        real, imag = values[:8], pltpu.roll(values[8:], 64, 1)
        d[t] = real - imag
        e[t] = real + imag
        return carry

    lax.fori_loop(0, frames, split, 0, unroll=8)

    def step(t, sums):
        return tuple(
            tuple(part[lag] + source[t] * source[t + lag] for lag in range(LAGS))
            for part, source in zip(sums, (d, e))
        )

    zero = (jnp.zeros((8, 128), jnp.float32),) * LAGS
    sums_d, sums_e = lax.fori_loop(0, frames, step, (zero, zero), unroll=8)
    for lag in range(LAGS):
        value = (sums_d[lag] + pltpu.roll(sums_e[lag], 64, 1)) * (1.0 / (ATOMS * (frames - lag)))
        rows[lag * 8 : lag * 8 + 8, :] = value

    _, upper, t = place()
    lane = lax.broadcasted_iota(jnp.int32, (128, 128), 1)
    comp, q = (lane // 32) * 16, lane % 32
    falling, rising = comp + 15 - q, comp + q - 16
    source = jnp.where(q < 16, 64 * upper + falling, 64 * (1 - upper) + rising)
    rows[...] = jnp.take_along_axis(rows[...], source, axis=1)
    flip = t % 4 < 2
    group = lax.broadcasted_iota(jnp.int32, (LAGS, 128), 1) // 32

    def wave(w):
        return rows[pl.ds(w, LAGS, stride=8), :]

    for half in range(2):
        totals = [jnp.zeros((LAGS, 128), jnp.float32) for _ in range(4)]
        for part in range(4):
            w = half * 4 + part
            value = jnp.where(flip, wave(7 - w), wave(w))
            for comp in range(4):
                by = (32 * (part - comp)) % 128
                moved = pltpu.roll(value, by, 1) if by else value
                totals[comp] = jnp.where(group == part, moved, totals[comp])
        for comp in range(4):
            out[comp, :, half * 128 : half * 128 + 128] = totals[comp]


def correlate(series):
    vmem = pl.BlockSpec(memory_space=pltpu.VMEM)
    return pl.pallas_call(
        correlate_kernel,
        out_shape=jax.ShapeDtypeStruct((4, LAGS, 256), jnp.float32),
        in_specs=[vmem],
        out_specs=vmem,
        scratch_shapes=[
            pltpu.VMEM((FRAMES + LAGS, 8, 128), jnp.float32),
            pltpu.VMEM((FRAMES + LAGS, 8, 128), jnp.float32),
            pltpu.VMEM((128, 128), jnp.float32),
        ],
        compiler_params=pltpu.CompilerParams(vmem_limit_bytes=GRANT),
        name="correlate",
    )(series)


def across(block):
    return lax.ppermute(block, "atom", [(i, i ^ 2) for i in range(8)])


def swap(block):
    return lax.ppermute(block, "atom", [(i, i ^ 1) for i in range(8)])


def exchange(local):
    groups = [[a * 16 + t for a in (lower, 7 - lower) for t in range(16)] for lower in range(4)]
    series = lax.all_to_all(
        local, ("atom", "tm"), 0, 0, tiled=True, axis_index_groups=groups
    )
    return series.reshape(2, FRAMES, 16, 128)


def per_device(positions, velocity):
    own = prepare(positions, velocity)
    other = across(own)
    sums = modes([own, swap(own)])
    other, sums = lax.optimization_barrier((other, sums))
    behind = swap(other)
    sums = modes([other], sums)
    return correlate(exchange(modes([behind], sums, True)))


def solution(mesh):
    in_specs = (P("tm", None, "atom"), P("tm", None, "atom"))
    out_specs = P(None, None, ("atom", "tm"))
    return jax.shard_map(
        per_device, mesh=mesh, in_specs=in_specs, out_specs=out_specs, check_vma=False
    )
```

```python
import functools
import math

import jax
import jax.numpy as jnp
from jax import lax
from jax.experimental import pallas as pl
from jax.experimental.pallas import tpu as pltpu
from jax.sharding import PartitionSpec as P

KX = 32
KY = 32
KZ = 32
LAGS = 16
LATTICE = 131072
ATOMS = 16384
FRAMES = 128
HALF = 16
LINK = jnp.bfloat16
WIDTH = 2
SPREAD = 136
GRANT = 16 << 20
ROWS = 75
SINE = (6.28318516, -41.3416550, 81.6010040, -76.5498338, 39.5367090)


def place():
    a, t = lax.axis_index("atom"), lax.axis_index("tm")
    return jnp.maximum(a, 7 - a), (a >= 4).astype(jnp.int32), t


def sine(u):
    square = u * u
    value = jnp.full_like(u, SINE[4])
    for factor in SINE[3::-1]:
        value = value * square + factor
    return value * u


def cos_sin(turns):
    r = turns - jnp.round(turns)
    c = sine(0.25 - jnp.abs(r))
    s = sine(jnp.maximum(jnp.minimum(r, 0.5 - r), -0.5 - r))
    return c, s


def harmonics(here, before, twice, number):
    values = [here]
    for _ in range(number - 1):
        values.append(twice * values[-1] - before)
        before = values[-2]
    return values


def fill(data, first, table):
    def put(row, values):
        for k, value in enumerate(values):
            table[pl.ds(row + k, 16, stride=ROWS), :] = value

    x, y, z = (
        (data[2 * a].astype(jnp.float32) * 512.0 + data[2 * a + 1].astype(jnp.float32))
        * (1.0 / LATTICE)
        for a in range(3)
    )
    c, s = cos_sin(x * first)
    c1, s1 = cos_sin(x)
    for i in range(4):
        put(2 * i, [c, s])
        if i < 3:
            c, s = c * c1 - s * s1, c * s1 + s * c1
    for row, angle in ((8, y), (40, z)):
        c1, s1 = cos_sin(angle)
        put(row, harmonics(c1, jnp.ones_like(c1), c1 + c1, HALF))
        put(row + HALF, harmonics(s1, jnp.zeros_like(s1), c1 + c1, HALF))
    put(72, [data[6 + comp].astype(jnp.float32) for comp in range(3)])


def prepare_kernel(far_positions, far_velocity, out, positions, velocity, spread, sem):
    frames = positions.shape[1]
    copies = [
        pltpu.make_async_copy(far_positions, positions, sem.at[0]),
        pltpu.make_async_copy(far_velocity, velocity, sem.at[1]),
    ]
    for copy in copies:
        copy.start()
    for copy in copies:
        copy.wait()
    for g in range(16):
        lanes = slice(g * 128, (g + 1) * 128)
        for a in range(3):
            whole = positions[a, :, lanes]
            low = ((whole + 256) & 511) - 256
            high = (whole - low) >> 9
            parts = (high, low, velocity[a, :, lanes])
            for k, part in zip((2 * a, 2 * a + 1, 6 + a), parts):
                spread[pl.ds(k * SPREAD + g, frames, stride=17), :] = part.astype(jnp.float32)
    for f in range(frames):
        for k in range(9):
            at = k * SPREAD + 17 * f
            out[f, k] = spread[at : at + 16, :].astype(jnp.bfloat16)


def prepare(positions, velocity):
    frames = positions.shape[0]
    vmem = pl.BlockSpec(memory_space=pltpu.VMEM)
    return pl.pallas_call(
        prepare_kernel,
        out_shape=jax.ShapeDtypeStruct((frames, 9, 16, 128), jnp.bfloat16),
        in_specs=[pl.BlockSpec(memory_space=pltpu.HBM)] * 2,
        out_specs=vmem,
        scratch_shapes=[
            pltpu.VMEM((3, frames, 2048), jnp.int32),
            pltpu.VMEM((3, frames, 2048), jnp.bfloat16),
            pltpu.VMEM((9 * SPREAD, 128), jnp.float32),
            pltpu.SemaphoreType.DMA((2,)),
        ],
        compiler_params=pltpu.CompilerParams(vmem_limit_bytes=GRANT),
        name="prepare",
    )(
        *(
            pltpu.with_memory_space_constraint(jnp.transpose(x, (1, 0, 2)), pltpu.HBM)
            for x in (positions, velocity)
        )
    )


def multiply(table, total):
    for start in range(0, 16, WIDTH):
        bases = [(start + k) * ROWS for k in range(WIDTH)]

        def rows(start, number):
            return [table[pl.ds(base + start, number), :] for base in bases]

        def wide(parts):
            return jnp.concatenate([p.astype(jnp.bfloat16) for p in parts], 1)

        yc = [rows(8 + 8 * b, 8) for b in range(2)]
        ys = [rows(24 + 8 * b, 8) for b in range(2)]
        left = []
        for i in range(4):
            cx, sx = rows(2 * i, 1), rows(2 * i + 1, 1)
            for b in range(2):
                plus, minus = [], []
                for k in range(WIDTH):
                    cc, sn = cx[k] * yc[b][k], sx[k] * ys[b][k]
                    cn, sc = cx[k] * ys[b][k], sx[k] * yc[b][k]
                    plus.append(jnp.concatenate([cc - sn, cn + sc], 0))
                    minus.append(jnp.concatenate([cc + sn, sc - cn], 0))
                left += [wide(plus), wide(minus)]
        right = []
        for part in range(2):
            z = rows(40 + 16 * part, 16)
            right.append(wide(z))
            for comp in range(3):
                u = rows(72 + comp, 1)
                right.append(wide([z[k] * u[k] for k in range(WIDTH)]))
        total = total + lax.dot_general(
            jnp.concatenate(left, 0),
            jnp.concatenate(right, 0),
            (((1,), (1,)), ((), ())),
            preferred_element_type=jnp.float32,
        )
    return total


def modes_kernel(number, frames, more, last, *refs):
    data, refs = refs[:number], refs[number:]
    if more:
        before, refs = refs[0], refs[1:]
    out, table_a, table_b, blocks, *rest = refs
    totals = rest[0] if last else out
    first = (4 * place()[0] - 15).astype(jnp.float32)
    steps = number * frames
    for g in range(number):
        for f in range(frames):
            blocks[g * frames + f] = data[g][f]

    def block(index):
        return [blocks[index, k] for k in range(9)]

    totals[...] = before[...] if more else jnp.zeros_like(totals)
    fill(block(0), first, table_a)

    def step(half, carry):
        now = 2 * half
        frame = now % frames
        fill(block(now + 1), first, table_b)
        totals[frame] = multiply(table_a, totals[frame])
        fill(block(jnp.minimum(now + 2, steps - 1)), first, table_a)
        totals[frame + 1] = multiply(table_b, totals[frame + 1])
        return carry

    lax.fori_loop(0, steps // 2, step, 0)
    if not last:
        return
    for f in range(frames):
        total = totals[f].astype(LINK)
        for i in range(4):
            for b in range(4):
                minus, outer = b < 2, b in (0, 3)
                here = 64 * i + 32 * outer + 16 * minus
                there = 64 * (3 - i) + 32 * outer + 16 * (not minus)
                out[i * 4 + b, f] = total[there : there + 16]
                out[16 + i * 4 + b, f] = total[here : here + 16]


def modes(blocks, before=None, last=False):
    frames = blocks[0].shape[0]
    number, more = len(blocks), before is not None
    vmem = pl.BlockSpec(memory_space=pltpu.VMEM)
    sums = (frames, 256, 128)
    work = number * frames * 2048
    return pl.pallas_call(
        functools.partial(modes_kernel, number, frames, more, last),
        out_shape=jax.ShapeDtypeStruct((32, frames, 16, 128), LINK)
        if last
        else jax.ShapeDtypeStruct(sums, jnp.float32),
        in_specs=[vmem] * (number + more),
        out_specs=vmem,
        scratch_shapes=[
            pltpu.VMEM((16 * ROWS, 128), jnp.float32),
            pltpu.VMEM((16 * ROWS, 128), jnp.float32),
            pltpu.VMEM((number * frames, 9, 16, 128), jnp.bfloat16),
        ]
        + [pltpu.VMEM(sums, jnp.float32)] * last,
        input_output_aliases={number: 0} if more and not last else {},
        cost_estimate=pl.CostEstimate(
            flops=work * 256 * 128 * 2, bytes_accessed=work * 18, transcendentals=0
        ),
        compiler_params=pltpu.CompilerParams(vmem_limit_bytes=GRANT),
        name="last" if last else f"nearby{int(more)}",
    )(*blocks, *([before] * more))


def correlate_kernel(series, out, d, e, rows):
    frames = FRAMES
    d[frames:, :, :] = jnp.zeros((LAGS, 8, 128), jnp.float32)
    e[frames:, :, :] = jnp.zeros((LAGS, 8, 128), jnp.float32)

    def split(t, carry):
        values = series[0, t].astype(jnp.float32) + series[1, t].astype(jnp.float32)
        real, imag = values[:8], pltpu.roll(values[8:], 64, 1)
        d[t] = real - imag
        e[t] = real + imag
        return carry

    lax.fori_loop(0, frames, split, 0, unroll=64)

    def step(t, sums):
        return tuple(
            tuple(part[lag] + source[t] * source[t + lag] for lag in range(LAGS))
            for part, source in zip(sums, (d, e))
        )

    zero = (jnp.zeros((8, 128), jnp.float32),) * LAGS
    sums_d, sums_e = lax.fori_loop(0, frames, step, (zero, zero), unroll=16)
    for lag in range(LAGS):
        value = (sums_d[lag] + pltpu.roll(sums_e[lag], 64, 1)) * (1.0 / (ATOMS * (frames - lag)))
        rows[lag * 8 : lag * 8 + 8, :] = value

    _, upper, t = place()
    lane = lax.broadcasted_iota(jnp.int32, (128, 128), 1)
    comp, q = (lane // 32) * 16, lane % 32
    falling, rising = comp + 15 - q, comp + q - 16
    source = jnp.where(q < 16, 64 * upper + falling, 64 * (1 - upper) + rising)
    rows[...] = jnp.take_along_axis(rows[...], source, axis=1)
    flip = t % 4 < 2
    group = lax.broadcasted_iota(jnp.int32, (LAGS, 128), 1) // 32

    def wave(w):
        return rows[pl.ds(w, LAGS, stride=8), :]

    for half in range(2):
        totals = [jnp.zeros((LAGS, 128), jnp.float32) for _ in range(4)]
        for part in range(4):
            w = half * 4 + part
            value = jnp.where(flip, wave(7 - w), wave(w))
            for comp in range(4):
                by = (32 * (part - comp)) % 128
                moved = pltpu.roll(value, by, 1) if by else value
                totals[comp] = jnp.where(group == part, moved, totals[comp])
        for comp in range(4):
            out[comp, :, half * 128 : half * 128 + 128] = totals[comp]


def correlate(series):
    vmem = pl.BlockSpec(memory_space=pltpu.VMEM)
    return pl.pallas_call(
        correlate_kernel,
        out_shape=jax.ShapeDtypeStruct((4, LAGS, 256), jnp.float32),
        in_specs=[vmem],
        out_specs=vmem,
        scratch_shapes=[
            pltpu.VMEM((FRAMES + LAGS, 8, 128), jnp.float32),
            pltpu.VMEM((FRAMES + LAGS, 8, 128), jnp.float32),
            pltpu.VMEM((128, 128), jnp.float32),
        ],
        compiler_params=pltpu.CompilerParams(vmem_limit_bytes=GRANT),
        name="correlate",
    )(series)


def across(block):
    return lax.ppermute(block, "atom", [(i, i ^ 2) for i in range(8)])


def swap(block):
    return lax.ppermute(block, "atom", [(i, i ^ 1) for i in range(8)])


def exchange(local):
    groups = [[a * 16 + t for a in (lower, 7 - lower) for t in range(16)] for lower in range(4)]
    series = lax.all_to_all(
        local, ("atom", "tm"), 0, 0, tiled=True, axis_index_groups=groups
    )
    return series.reshape(2, FRAMES, 16, 128)


def per_device(positions, velocity):
    own = prepare(positions, velocity)
    other = across(own)
    sums = modes([own, swap(own)])
    other, sums = lax.optimization_barrier((other, sums))
    behind = swap(other)
    sums = modes([other], sums)
    return correlate(exchange(modes([behind], sums, True)))


def solution(mesh):
    in_specs = (P("tm", None, "atom"), P("tm", None, "atom"))
    out_specs = P(None, None, ("atom", "tm"))
    return jax.shard_map(
        per_device, mesh=mesh, in_specs=in_specs, out_specs=out_specs, check_vma=False
    )
```

```python
import functools
import math

import jax
import jax.numpy as jnp
from jax import lax
from jax.experimental import pallas as pl
from jax.experimental.pallas import tpu as pltpu
from jax.sharding import PartitionSpec as P

KX = 32
KY = 32
KZ = 32
LAGS = 16
LATTICE = 131072
ATOMS = 16384
FRAMES = 128
HALF = 16
ORDER = (26, 17, 11, 10, 28, 1, 5, 4, 7, 16, 9, 19, 30, 13, 22, 0, 21, 29, 6, 12, 20, 23, 14, 15, 3, 31, 2, 24, 25, 27, 18, 8)
LINK = jnp.bfloat16
WIDTH = 2
SPREAD = 136
GRANT = 16 << 20
ROWS = 75
SINE = (6.28318516, -41.3416550, 81.6010040, -76.5498338, 39.5367090)


def place():
    a, t = lax.axis_index("atom"), lax.axis_index("tm")
    return jnp.maximum(a, 7 - a), (a >= 4).astype(jnp.int32), t


def sine(u):
    square = u * u
    value = jnp.full_like(u, SINE[4])
    for factor in SINE[3::-1]:
        value = value * square + factor
    return value * u


def cos_sin(turns):
    r = turns - jnp.round(turns)
    c = sine(0.25 - jnp.abs(r))
    s = sine(jnp.maximum(jnp.minimum(r, 0.5 - r), -0.5 - r))
    return c, s


def harmonics(here, before, twice, number):
    values = [here]
    for _ in range(number - 1):
        values.append(twice * values[-1] - before)
        before = values[-2]
    return values


def fill(data, first, table):
    def put(row, values):
        for k, value in enumerate(values):
            table[pl.ds(row + k, 16, stride=ROWS), :] = value

    x, y, z = (
        (data[2 * a].astype(jnp.float32) * 512.0 + data[2 * a + 1].astype(jnp.float32))
        * (1.0 / LATTICE)
        for a in range(3)
    )
    c, s = cos_sin(x * first)
    c1, s1 = cos_sin(x)
    for i in range(4):
        put(2 * i, [c, s])
        if i < 3:
            c, s = c * c1 - s * s1, c * s1 + s * c1
    for row, angle in ((8, y), (40, z)):
        c1, s1 = cos_sin(angle)
        put(row, harmonics(c1, jnp.ones_like(c1), c1 + c1, HALF))
        put(row + HALF, harmonics(s1, jnp.zeros_like(s1), c1 + c1, HALF))
    put(72, [data[6 + comp].astype(jnp.float32) for comp in range(3)])


def prepare_kernel(far_positions, far_velocity, out, positions, velocity, spread, sem):
    frames = positions.shape[1]
    copies = [
        pltpu.make_async_copy(far_positions, positions, sem.at[0]),
        pltpu.make_async_copy(far_velocity, velocity, sem.at[1]),
    ]
    for copy in copies:
        copy.start()
    for copy in copies:
        copy.wait()
    for g in range(16):
        lanes = slice(g * 128, (g + 1) * 128)
        for a in range(3):
            whole = positions[a, :, lanes]
            low = ((whole + 256) & 511) - 256
            high = (whole - low) >> 9
            parts = (high, low, velocity[a, :, lanes])
            for k, part in zip((2 * a, 2 * a + 1, 6 + a), parts):
                spread[pl.ds(k * SPREAD + g, frames, stride=17), :] = part.astype(jnp.float32)
    for f in range(frames):
        for k in range(9):
            at = k * SPREAD + 17 * f
            out[f, k] = spread[at : at + 16, :].astype(jnp.bfloat16)


def prepare(positions, velocity):
    frames = positions.shape[0]
    vmem = pl.BlockSpec(memory_space=pltpu.VMEM)
    return pl.pallas_call(
        prepare_kernel,
        out_shape=jax.ShapeDtypeStruct((frames, 9, 16, 128), jnp.bfloat16),
        in_specs=[pl.BlockSpec(memory_space=pltpu.HBM)] * 2,
        out_specs=vmem,
        scratch_shapes=[
            pltpu.VMEM((3, frames, 2048), jnp.int32),
            pltpu.VMEM((3, frames, 2048), jnp.bfloat16),
            pltpu.VMEM((9 * SPREAD, 128), jnp.float32),
            pltpu.SemaphoreType.DMA((2,)),
        ],
        compiler_params=pltpu.CompilerParams(vmem_limit_bytes=GRANT),
        name="prepare",
    )(
        *(
            pltpu.with_memory_space_constraint(jnp.transpose(x, (1, 0, 2)), pltpu.HBM)
            for x in (positions, velocity)
        )
    )


def multiply(table, total):
    for start in range(0, 16, WIDTH):
        bases = [(start + k) * ROWS for k in range(WIDTH)]

        def rows(start, number):
            return [table[pl.ds(base + start, number), :] for base in bases]

        def wide(parts):
            return jnp.concatenate([p.astype(jnp.bfloat16) for p in parts], 1)

        yc = [rows(8 + 8 * b, 8) for b in range(2)]
        ys = [rows(24 + 8 * b, 8) for b in range(2)]
        left = []
        for i in range(4):
            cx, sx = rows(2 * i, 1), rows(2 * i + 1, 1)
            for b in range(2):
                plus, minus = [], []
                for k in range(WIDTH):
                    cc, sn = cx[k] * yc[b][k], sx[k] * ys[b][k]
                    cn, sc = cx[k] * ys[b][k], sx[k] * yc[b][k]
                    plus.append(jnp.concatenate([cc - sn, cn + sc], 0))
                    minus.append(jnp.concatenate([cc + sn, sc - cn], 0))
                left += [wide(plus), wide(minus)]
        right = []
        for part in range(2):
            z = rows(40 + 16 * part, 16)
            right.append(wide(z))
            for comp in range(3):
                u = rows(72 + comp, 1)
                right.append(wide([z[k] * u[k] for k in range(WIDTH)]))
        total = total + lax.dot_general(
            jnp.concatenate(left, 0),
            jnp.concatenate(right, 0),
            (((1,), (1,)), ((), ())),
            preferred_element_type=jnp.float32,
        )
    return total


def modes_kernel(number, frames, more, last, *refs):
    data, refs = refs[:number], refs[number:]
    if more:
        before, refs = refs[0], refs[1:]
    out, table_a, table_b, blocks, *rest = refs
    totals = rest[0] if last else out
    first = (4 * place()[0] - 15).astype(jnp.float32)
    steps = number * frames
    for g in range(number):
        for f in range(frames):
            blocks[g * frames + f] = data[g][f]

    def block(index):
        return [blocks[index, k] for k in range(9)]

    totals[...] = before[...] if more else jnp.zeros_like(totals)
    fill(block(0), first, table_a)

    def step(half, carry):
        now = 2 * half
        frame = now % frames
        fill(block(now + 1), first, table_b)
        totals[frame] = multiply(table_a, totals[frame])
        fill(block(jnp.minimum(now + 2, steps - 1)), first, table_a)
        totals[frame + 1] = multiply(table_b, totals[frame + 1])
        return carry

    lax.fori_loop(0, steps // 2, step, 0)
    if not last:
        return
    for f in range(frames):
        total = totals[f].astype(LINK)
        for i in range(4):
            for b in range(4):
                minus, outer = b < 2, b in (0, 3)
                here = 64 * i + 32 * outer + 16 * minus
                there = 64 * (3 - i) + 32 * outer + 16 * (not minus)
                out[ORDER.index(i * 4 + b), f] = total[there : there + 16]
                out[ORDER.index(16 + i * 4 + b), f] = total[here : here + 16]


def modes(blocks, before=None, last=False):
    frames = blocks[0].shape[0]
    number, more = len(blocks), before is not None
    vmem = pl.BlockSpec(memory_space=pltpu.VMEM)
    sums = (frames, 256, 128)
    work = number * frames * 2048
    return pl.pallas_call(
        functools.partial(modes_kernel, number, frames, more, last),
        out_shape=jax.ShapeDtypeStruct((32, frames, 16, 128), LINK)
        if last
        else jax.ShapeDtypeStruct(sums, jnp.float32),
        in_specs=[vmem] * (number + more),
        out_specs=vmem,
        scratch_shapes=[
            pltpu.VMEM((16 * ROWS, 128), jnp.float32),
            pltpu.VMEM((16 * ROWS, 128), jnp.float32),
            pltpu.VMEM((number * frames, 9, 16, 128), jnp.bfloat16),
        ]
        + [pltpu.VMEM(sums, jnp.float32)] * last,
        input_output_aliases={number: 0} if more and not last else {},
        cost_estimate=pl.CostEstimate(
            flops=work * 256 * 128 * 2, bytes_accessed=work * 18, transcendentals=0
        ),
        compiler_params=pltpu.CompilerParams(vmem_limit_bytes=GRANT),
        name="last" if last else f"nearby{int(more)}",
    )(*blocks, *([before] * more))


def correlate_kernel(series, out, d, e, rows):
    frames = FRAMES
    d[frames:, :, :] = jnp.zeros((LAGS, 8, 128), jnp.float32)
    e[frames:, :, :] = jnp.zeros((LAGS, 8, 128), jnp.float32)

    for t in range(frames):
        source, f = divmod(t, series.shape[1])
        values = sum(
            series[ORDER.index(side * 16 + source), f].astype(jnp.float32) for side in range(2)
        )
        real, imag = values[:8], pltpu.roll(values[8:], 64, 1)
        d[t] = real - imag
        e[t] = real + imag

    def step(t, sums):
        return tuple(
            tuple(part[lag] + source[t] * source[t + lag] for lag in range(LAGS))
            for part, source in zip(sums, (d, e))
        )

    zero = (jnp.zeros((8, 128), jnp.float32),) * LAGS
    sums_d, sums_e = lax.fori_loop(0, frames, step, (zero, zero), unroll=16)
    for lag in range(LAGS):
        value = (sums_d[lag] + pltpu.roll(sums_e[lag], 64, 1)) * (1.0 / (ATOMS * (frames - lag)))
        rows[lag * 8 : lag * 8 + 8, :] = value

    _, upper, t = place()
    lane = lax.broadcasted_iota(jnp.int32, (128, 128), 1)
    comp, q = (lane // 32) * 16, lane % 32
    falling, rising = comp + 15 - q, comp + q - 16
    source = jnp.where(q < 16, 64 * upper + falling, 64 * (1 - upper) + rising)
    rows[...] = jnp.take_along_axis(rows[...], source, axis=1)
    flip = t % 4 < 2
    group = lax.broadcasted_iota(jnp.int32, (LAGS, 128), 1) // 32

    def wave(w):
        return rows[pl.ds(w, LAGS, stride=8), :]

    for half in range(2):
        totals = [jnp.zeros((LAGS, 128), jnp.float32) for _ in range(4)]
        for part in range(4):
            w = half * 4 + part
            value = jnp.where(flip, wave(7 - w), wave(w))
            for comp in range(4):
                by = (32 * (part - comp)) % 128
                moved = pltpu.roll(value, by, 1) if by else value
                totals[comp] = jnp.where(group == part, moved, totals[comp])
        for comp in range(4):
            out[comp, :, half * 128 : half * 128 + 128] = totals[comp]


def correlate(series):
    vmem = pl.BlockSpec(memory_space=pltpu.VMEM)
    return pl.pallas_call(
        correlate_kernel,
        out_shape=jax.ShapeDtypeStruct((4, LAGS, 256), jnp.float32),
        in_specs=[vmem],
        out_specs=vmem,
        scratch_shapes=[
            pltpu.VMEM((FRAMES + LAGS, 8, 128), jnp.float32),
            pltpu.VMEM((FRAMES + LAGS, 8, 128), jnp.float32),
            pltpu.VMEM((128, 128), jnp.float32),
        ],
        compiler_params=pltpu.CompilerParams(vmem_limit_bytes=GRANT),
        name="correlate",
    )(series)


def across(block):
    return lax.ppermute(block, "atom", [(i, i ^ 2) for i in range(8)])


def swap(block):
    return lax.ppermute(block, "atom", [(i, i ^ 1) for i in range(8)])


def exchange(local):
    groups = [
        [(7 - lower if at // 16 else lower) * 16 + at % 16 for at in ORDER] for lower in range(4)
    ]
    return lax.all_to_all(local, ("atom", "tm"), 0, 0, tiled=True, axis_index_groups=groups)


def per_device(positions, velocity):
    own = prepare(positions, velocity)
    other = across(own)
    sums = modes([own, swap(own)])
    other, sums = lax.optimization_barrier((other, sums))
    behind = swap(other)
    sums = modes([other], sums)
    return correlate(exchange(modes([behind], sums, True)))


def solution(mesh):
    in_specs = (P("tm", None, "atom"), P("tm", None, "atom"))
    out_specs = P(None, None, ("atom", "tm"))
    return jax.shard_map(
        per_device, mesh=mesh, in_specs=in_specs, out_specs=out_specs, check_vma=False
    )
```

```python
import functools
import math

import jax
import jax.numpy as jnp
from jax import lax
from jax.experimental import pallas as pl
from jax.experimental.pallas import tpu as pltpu
from jax.sharding import PartitionSpec as P

KX = 32
KY = 32
KZ = 32
LAGS = 16
LATTICE = 131072
ATOMS = 16384
FRAMES = 128
HALF = 16
ORDER = (27, 11, 0, 13, 29, 25, 31, 18, 17, 10, 5, 3, 4, 1, 15, 26, 12, 30, 21, 14, 2, 9, 28, 23, 8, 7, 16, 20, 24, 22, 19, 6)
LINK = jnp.bfloat16
WIDTH = 2
SPREAD = 136
GRANT = 16 << 20
ROWS = 75
SINE = (6.28318516, -41.3416550, 81.6010040, -76.5498338, 39.5367090)


def place():
    a, t = lax.axis_index("atom"), lax.axis_index("tm")
    return jnp.maximum(a, 7 - a), (a >= 4).astype(jnp.int32), t


def sine(u):
    square = u * u
    value = jnp.full_like(u, SINE[4])
    for factor in SINE[3::-1]:
        value = value * square + factor
    return value * u


def cos_sin(turns):
    r = turns - jnp.round(turns)
    c = sine(0.25 - jnp.abs(r))
    s = sine(jnp.maximum(jnp.minimum(r, 0.5 - r), -0.5 - r))
    return c, s


def harmonics(here, before, twice, number):
    values = [here]
    for _ in range(number - 1):
        values.append(twice * values[-1] - before)
        before = values[-2]
    return values


def fill(data, first, table):
    def put(row, values):
        for k, value in enumerate(values):
            table[pl.ds(row + k, 16, stride=ROWS), :] = value

    x, y, z = (
        (data[2 * a].astype(jnp.float32) * 512.0 + data[2 * a + 1].astype(jnp.float32))
        * (1.0 / LATTICE)
        for a in range(3)
    )
    c, s = cos_sin(x * first)
    c1, s1 = cos_sin(x)
    for i in range(4):
        put(2 * i, [c, s])
        if i < 3:
            c, s = c * c1 - s * s1, c * s1 + s * c1
    for row, angle in ((8, y), (40, z)):
        c1, s1 = cos_sin(angle)
        put(row, harmonics(c1, jnp.ones_like(c1), c1 + c1, HALF))
        put(row + HALF, harmonics(s1, jnp.zeros_like(s1), c1 + c1, HALF))
    put(72, [data[6 + comp].astype(jnp.float32) for comp in range(3)])


def prepare_kernel(far_positions, far_velocity, out, positions, velocity, spread, sem):
    frames = positions.shape[1]
    copies = [
        pltpu.make_async_copy(far_positions, positions, sem.at[0]),
        pltpu.make_async_copy(far_velocity, velocity, sem.at[1]),
    ]
    for copy in copies:
        copy.start()
    for copy in copies:
        copy.wait()
    for g in range(16):
        lanes = slice(g * 128, (g + 1) * 128)
        for a in range(3):
            whole = positions[a, :, lanes]
            low = ((whole + 256) & 511) - 256
            high = (whole - low) >> 9
            parts = (high, low, velocity[a, :, lanes])
            for k, part in zip((2 * a, 2 * a + 1, 6 + a), parts):
                spread[pl.ds(k * SPREAD + g, frames, stride=17), :] = part.astype(jnp.float32)
    for f in range(frames):
        for k in range(9):
            at = k * SPREAD + 17 * f
            out[f, k] = spread[at : at + 16, :].astype(jnp.bfloat16)


def prepare(positions, velocity):
    frames = positions.shape[0]
    vmem = pl.BlockSpec(memory_space=pltpu.VMEM)
    return pl.pallas_call(
        prepare_kernel,
        out_shape=jax.ShapeDtypeStruct((frames, 9, 16, 128), jnp.bfloat16),
        in_specs=[pl.BlockSpec(memory_space=pltpu.HBM)] * 2,
        out_specs=vmem,
        scratch_shapes=[
            pltpu.VMEM((3, frames, 2048), jnp.int32),
            pltpu.VMEM((3, frames, 2048), jnp.bfloat16),
            pltpu.VMEM((9 * SPREAD, 128), jnp.float32),
            pltpu.SemaphoreType.DMA((2,)),
        ],
        compiler_params=pltpu.CompilerParams(vmem_limit_bytes=GRANT),
        name="prepare",
    )(
        *(
            pltpu.with_memory_space_constraint(jnp.transpose(x, (1, 0, 2)), pltpu.HBM)
            for x in (positions, velocity)
        )
    )


def multiply(table, total):
    for start in range(0, 16, WIDTH):
        bases = [(start + k) * ROWS for k in range(WIDTH)]

        def rows(start, number):
            return [table[pl.ds(base + start, number), :] for base in bases]

        def wide(parts):
            return jnp.concatenate([p.astype(jnp.bfloat16) for p in parts], 1)

        yc = [rows(8 + 8 * b, 8) for b in range(2)]
        ys = [rows(24 + 8 * b, 8) for b in range(2)]
        left = []
        for i in range(4):
            cx, sx = rows(2 * i, 1), rows(2 * i + 1, 1)
            for b in range(2):
                plus, minus = [], []
                for k in range(WIDTH):
                    cc, sn = cx[k] * yc[b][k], sx[k] * ys[b][k]
                    cn, sc = cx[k] * ys[b][k], sx[k] * yc[b][k]
                    plus.append(jnp.concatenate([cc - sn, cn + sc], 0))
                    minus.append(jnp.concatenate([cc + sn, sc - cn], 0))
                left += [wide(plus), wide(minus)]
        right = []
        for part in range(2):
            z = rows(40 + 16 * part, 16)
            right.append(wide(z))
            for comp in range(3):
                u = rows(72 + comp, 1)
                right.append(wide([z[k] * u[k] for k in range(WIDTH)]))
        total = total + lax.dot_general(
            jnp.concatenate(left, 0),
            jnp.concatenate(right, 0),
            (((1,), (1,)), ((), ())),
            preferred_element_type=jnp.float32,
        )
    return total


def modes_kernel(number, frames, more, last, *refs):
    data, refs = refs[:number], refs[number:]
    if more:
        before, refs = refs[0], refs[1:]
    out, table_a, table_b, blocks, *rest = refs
    totals = rest[0] if last else out
    first = (4 * place()[0] - 15).astype(jnp.float32)
    steps = number * frames
    for g in range(number):
        for f in range(frames):
            blocks[g * frames + f] = data[g][f]

    def block(index):
        return [blocks[index, k] for k in range(9)]

    totals[...] = before[...] if more else jnp.zeros_like(totals)
    fill(block(0), first, table_a)

    def step(half, carry):
        now = 2 * half
        frame = now % frames
        fill(block(now + 1), first, table_b)
        totals[frame] = multiply(table_a, totals[frame])
        fill(block(jnp.minimum(now + 2, steps - 1)), first, table_a)
        totals[frame + 1] = multiply(table_b, totals[frame + 1])
        return carry

    lax.fori_loop(0, steps // 2, step, 0)
    if not last:
        return
    for f in range(frames):
        total = totals[f].astype(LINK)
        for i in range(4):
            for b in range(4):
                minus, outer = b < 2, b in (0, 3)
                here = 64 * i + 32 * outer + 16 * minus
                there = 64 * (3 - i) + 32 * outer + 16 * (not minus)
                out[ORDER.index(i * 4 + b), f] = total[there : there + 16]
                out[ORDER.index(16 + i * 4 + b), f] = total[here : here + 16]


def modes(blocks, before=None, last=False):
    frames = blocks[0].shape[0]
    number, more = len(blocks), before is not None
    vmem = pl.BlockSpec(memory_space=pltpu.VMEM)
    sums = (frames, 256, 128)
    work = number * frames * 2048
    return pl.pallas_call(
        functools.partial(modes_kernel, number, frames, more, last),
        out_shape=jax.ShapeDtypeStruct((32, frames, 16, 128), LINK)
        if last
        else jax.ShapeDtypeStruct(sums, jnp.float32),
        in_specs=[vmem] * (number + more),
        out_specs=vmem,
        scratch_shapes=[
            pltpu.VMEM((16 * ROWS, 128), jnp.float32),
            pltpu.VMEM((16 * ROWS, 128), jnp.float32),
            pltpu.VMEM((number * frames, 9, 16, 128), jnp.bfloat16),
        ]
        + [pltpu.VMEM(sums, jnp.float32)] * last,
        input_output_aliases={number: 0} if more and not last else {},
        cost_estimate=pl.CostEstimate(
            flops=work * 256 * 128 * 2, bytes_accessed=work * 18, transcendentals=0
        ),
        compiler_params=pltpu.CompilerParams(vmem_limit_bytes=GRANT),
        name="last" if last else f"nearby{int(more)}",
    )(*blocks, *([before] * more))


def correlate_kernel(series, out, d, e, rows):
    frames = FRAMES
    d[frames:, :, :] = jnp.zeros((LAGS, 8, 128), jnp.float32)
    e[frames:, :, :] = jnp.zeros((LAGS, 8, 128), jnp.float32)

    for t in range(frames):
        source, f = divmod(t, series.shape[1])
        values = sum(
            series[ORDER.index(side * 16 + source), f].astype(jnp.float32) for side in range(2)
        )
        real, imag = values[:8], pltpu.roll(values[8:], 64, 1)
        d[t] = real - imag
        e[t] = real + imag

    def step(t, sums):
        return tuple(
            tuple(part[lag] + source[t] * source[t + lag] for lag in range(LAGS))
            for part, source in zip(sums, (d, e))
        )

    zero = (jnp.zeros((8, 128), jnp.float32),) * LAGS
    sums_d, sums_e = lax.fori_loop(0, frames, step, (zero, zero), unroll=16)
    for lag in range(LAGS):
        value = (sums_d[lag] + pltpu.roll(sums_e[lag], 64, 1)) * (1.0 / (ATOMS * (frames - lag)))
        rows[lag * 8 : lag * 8 + 8, :] = value

    _, upper, t = place()
    lane = lax.broadcasted_iota(jnp.int32, (128, 128), 1)
    comp, q = (lane // 32) * 16, lane % 32
    falling, rising = comp + 15 - q, comp + q - 16
    source = jnp.where(q < 16, 64 * upper + falling, 64 * (1 - upper) + rising)
    rows[...] = jnp.take_along_axis(rows[...], source, axis=1)
    flip = t % 4 < 2
    group = lax.broadcasted_iota(jnp.int32, (LAGS, 128), 1) // 32

    def wave(w):
        return rows[pl.ds(w, LAGS, stride=8), :]

    for half in range(2):
        totals = [jnp.zeros((LAGS, 128), jnp.float32) for _ in range(4)]
        for part in range(4):
            w = half * 4 + part
            value = jnp.where(flip, wave(7 - w), wave(w))
            for comp in range(4):
                by = (32 * (part - comp)) % 128
                moved = pltpu.roll(value, by, 1) if by else value
                totals[comp] = jnp.where(group == part, moved, totals[comp])
        for comp in range(4):
            out[comp, :, half * 128 : half * 128 + 128] = totals[comp]


def correlate(series):
    vmem = pl.BlockSpec(memory_space=pltpu.VMEM)
    return pl.pallas_call(
        correlate_kernel,
        out_shape=jax.ShapeDtypeStruct((4, LAGS, 256), jnp.float32),
        in_specs=[vmem],
        out_specs=vmem,
        scratch_shapes=[
            pltpu.VMEM((FRAMES + LAGS, 8, 128), jnp.float32),
            pltpu.VMEM((FRAMES + LAGS, 8, 128), jnp.float32),
            pltpu.VMEM((128, 128), jnp.float32),
        ],
        compiler_params=pltpu.CompilerParams(vmem_limit_bytes=GRANT),
        name="correlate",
    )(series)


def across(block):
    return lax.ppermute(block, "atom", [(i, i ^ 2) for i in range(8)])


def swap(block):
    return lax.ppermute(block, "atom", [(i, i ^ 1) for i in range(8)])


def exchange(local):
    groups = [
        [(7 - lower if at // 16 else lower) * 16 + at % 16 for at in ORDER] for lower in range(4)
    ]
    return lax.all_to_all(local, ("atom", "tm"), 0, 0, tiled=True, axis_index_groups=groups)


def per_device(positions, velocity):
    own = prepare(positions, velocity)
    other = across(own)
    sums = modes([own, swap(own)])
    other, sums = lax.optimization_barrier((other, sums))
    behind = swap(other)
    sums = modes([other], sums)
    return correlate(exchange(modes([behind], sums, True)))


def solution(mesh):
    in_specs = (P("tm", None, "atom"), P("tm", None, "atom"))
    out_specs = P(None, None, ("atom", "tm"))
    return jax.shard_map(
        per_device, mesh=mesh, in_specs=in_specs, out_specs=out_specs, check_vma=False
    )
```
